128 devices in a mesh: row: 16 (over z_hi, x, core), col: 8 (over y, z_lo).
Axes of the slice: x: 4, y: 4, z: 4 (z_hi: 2, z_lo: 2; z = z_hi * 2 + z_lo), core: 2. Of those that a mesh axis runs over, the one named last changes fastest.
Arguments:
- struct_basis: float32 [32768, 1024], P(('row', 'col')), may hold values from -24 to 24
- fluid_basis: float32 [16384, 1024], P(('row', 'col')), may hold values from -24 to 24
- stiff_tiles: float32 [256, 4, 128, 128], P(('row', 'col')), may hold values from -0.0014648438 to 0.0014648438
- mass_tiles: float32 [256, 4, 128, 128], P(('row', 'col')), may hold values from -0.0014648438 to 0.0014648438
- fluid_stiff_tiles: float32 [128, 4, 128, 128], P(('row', 'col')), may hold values from -0.001953125 to 0.001953125
- fluid_mass_tiles: float32 [128, 4, 128, 128], P(('row', 'col')), may hold values from -0.001953125 to 0.001953125
- struct_cols: int32 [256, 4], P(('row', 'col')), may hold values from 0 to 3
- fluid_cols: int32 [128, 4], P(('row', 'col')), may hold values from 0 to 2
- wet_rows: int32 [16384], P(('row', 'col')), may hold values from 0 to 127
- wet_dest: int32 [16384, 1], P(('row', 'col')), may hold values from 0 to 127; in each aligned block of 128 rows (0 to 127, 128 to 255, ...) at most 2 rows name the same one
- coupling: float32 [32768, 256], P(('row', 'col')), may hold values from -0.001953125 to 0.001953125
Outputs:
- stiff_red: float32 [1024, 1024], P('row', 'col')
- mass_red: float32 [1024, 1024], P('row', 'col')
- fluid_stiff_red: float32 [1024, 1024], P('row', 'col')
- fluid_mass_red: float32 [1024, 1024], P('row', 'col')
- coupling_red: float32 [1024, 1024], P('row', 'col')
The draws below stay inside these ranges and needn't reach their ends.
Inputs may be any that keep to these rules, and one draw needn't show every extreme that they name: `wet_dest`: among the 128 entries of one block, no block number is named more than 2 times, and some block number is named exactly 2 times in every draw.
All inputs are finite; a program needn't handle non-finite values.
Results may differ from the reference program's by a relative error of at most 0.0003.
Values sent between devices are 32-bit elements; how exact they have to be, the bound alone decides.
No kernel may reach another device: no remote copies, remote signals or barrier semaphores. Data moves between devices by JAX's collectives and lax.ppermute only.
A program may use at most 128 MiB of HBM per device.

```python
import math
import jax
import jax.numpy as jnp
import numpy as np
from jax import lax

R = 1024
TILE = 128
NB = 4
HALO = 1
CAP = 2
STILE_DEV = 2
ATILE_DEV = 1
SHARDS = 128
WET_DEV = 128
AROWS_DEV = 128
NS = 32768
NA = 16384
NREC = 256
N_ROW = 16
N_COL = 8


def with_ends(values, key, low, largest):
    place = [jax.random.randint(jax.random.fold_in(key, axis), (), 0, length) for axis, length in enumerate(values.shape)]
    widest = values.shape.index(max(values.shape))
    neighbour = place[:widest] + [(place[widest] + 1) % values.shape[widest]] + place[widest + 1:]
    return values.at[tuple(place)].set(low).at[tuple(neighbour)].set(largest)


def with_spikes(entries, stream_key, source, target, blocks, factor):
    owner, partner = [(jnp.arange(entries.shape[axis_at]) // (entries.shape[axis_at] // blocks)).reshape([-1 if axis == axis_at else 1 for axis in range(entries.ndim)]) for axis_at in (source, target)]
    chosen = jax.random.permutation(stream_key, blocks)[partner]
    strong = (owner == chosen) | (owner == (partner + blocks // 2) % blocks)
    return jnp.where(strong, factor * entries, entries)


def block_levels(own_key, shape, cuts, least, high):
    level, own = 1.0, jax.random.fold_in(own_key, 6)
    for position, blocks in cuts:
        draws = jnp.exp(jax.random.uniform(jax.random.fold_in(own, position), (blocks,), jnp.float32, least / len(cuts), high / len(cuts)))
        level = level * jnp.repeat(draws, shape[position] // blocks).reshape([-1 if axis == position else 1 for axis in range(len(shape))])
    return level


def assign_block(stream_key, own, number, rows, count, top, bound, lean):
    order = jax.random.permutation(stream_key, count)
    packed, common = load_shares(count, rows * top, bound, lean, True), load_shares(count, rows * top, bound, lean, False)
    places = jnp.arange(count)

    def named(lengths, rotation):
        used = int((lengths > 0).sum())
        fixed = max(1, used // 4)
        moved = fixed + (places - fixed + rotation * (used - fixed)) % max(1, count - fixed)
        return jnp.zeros((count,), jnp.int32).at[order[jnp.where(places < fixed, places, moved)]].set(jnp.asarray(lengths, jnp.int32))

    lengths = jnp.where(number % 4 == 0, named(packed, number // 4), named(common, number - number // 4 - 1))
    mixed = jax.random.permutation(jax.random.fold_in(own, 3), count)
    donor, receiver = mixed[0:count // 2 * 2:2], mixed[1:count // 2 * 2:2]
    margin = jnp.minimum(lengths[donor] - 1, bound - lengths[receiver]) // 2
    margin = jnp.where((donor == order[0]) | (receiver == order[0]) | (lengths[receiver] == 0), 0, jnp.maximum(margin, 0))
    moved = jax.random.randint(jax.random.fold_in(own, 4), (count // 2,), 0, 1 << 20) % (margin + 1)
    lengths = lengths.at[donor].add(-moved).at[receiver].add(moved)
    labels = jnp.searchsorted(jnp.cumsum(lengths), jnp.arange(rows * top), side="right").astype(jnp.int32)
    table = labels.reshape(top, rows).T
    table = table[jax.random.permutation(jax.random.fold_in(own, 1), rows)]
    rotation = jax.random.randint(jax.random.fold_in(own, 2), (rows, 1), 0, top)
    return jnp.take_along_axis(table, (jnp.arange(top)[None, :] + rotation) % top, axis=1)


def load_shares(amount, total, limit, skew, full):
    loads = [(1 << 20) // math.isqrt(standing ** skew) + 1 for standing in range(1, amount + 1)]
    largest = limit if full else min(limit, max(-(-total // amount), total * loads[0] // sum(loads)))
    least = 1 if total - largest >= amount - 1 else 0
    given, rest = [largest] + [least] * (amount - 1), total - largest - least * (amount - 1)
    while rest > 0:
        candidates = [i for i in range(1, amount) if given[i] < largest] or [i for i in range(1, amount) if given[i] < limit]
        pool, budget = sum([loads[i] for i in candidates]), rest
        for i in candidates:
            extra = min(limit - given[i], max(1, budget * loads[i] // pool), rest)
            given[i] = given[i] + extra
            rest = rest - extra
    return np.array(given)


def noise(key, shape, deviation, most, shards=(), kind=jnp.bfloat16):
    values = jax.random.normal(key, shape, jnp.float32) * deviation
    if len(shards) > 0:
        values = block_levels(key, shape, shards, -0.22, 0.18) * values
    return jnp.clip(values, min=-most, max=most).astype(kind)


def noise_with(own_key, shape, scale, reach, shards, heavy, held_as=jnp.bfloat16):
    values = scale * jax.random.normal(own_key, shape, jnp.float32)
    if shards:
        values = values * block_levels(own_key, shape, shards, -0.22, 0.18)
    return jnp.clip(with_spikes(values, jax.random.fold_in(own_key, 3), *heavy), -reach, reach).astype(held_as)


def setup_inputs(seed: int = 0) -> dict:
    streams_of = jax.random.split(jax.random.key(seed), 12)
    struct_basis = noise_with(streams_of[0], (NS, R), 1.0, 24.0, ((0, 128),), (0, 1, 128, 5.5), jnp.float32)
    fluid_basis = noise_with(streams_of[1], (NA, R), 1.0, 24.0, ((0, 128),), (0, 1, 128, 5.5), jnp.float32)
    stiff_tiles = noise(streams_of[2], (STILE_DEV * SHARDS, NB, TILE, TILE), (TILE * NB * NS) ** -0.5, 0.0014648438, ((0, 128),), jnp.float32)
    mass_tiles = noise(streams_of[3], (STILE_DEV * SHARDS, NB, TILE, TILE), (TILE * NB * NS) ** -0.5, 0.0014648438, ((0, 128),), jnp.float32)
    fluid_stiff_tiles = noise(streams_of[4], (ATILE_DEV * SHARDS, NB, TILE, TILE), (TILE * NB * NA) ** -0.5, 0.001953125, ((0, 128),), jnp.float32)
    fluid_mass_tiles = noise(streams_of[5], (ATILE_DEV * SHARDS, NB, TILE, TILE), (TILE * NB * NA) ** -0.5, 0.001953125, ((0, 128),), jnp.float32)
    struct_cols = with_ends(jax.random.randint(streams_of[6], (STILE_DEV * SHARDS, NB), 0, STILE_DEV + 2 * HALO), jax.random.fold_in(streams_of[6], 1), 0, (STILE_DEV + 2 * HALO) - 1).astype(jnp.int32)
    fluid_cols = with_ends(jax.random.randint(streams_of[7], (ATILE_DEV * SHARDS, NB), 0, ATILE_DEV + 2 * HALO), jax.random.fold_in(streams_of[7], 1), 0, (ATILE_DEV + 2 * HALO) - 1).astype(jnp.int32)
    wet_rows = with_ends(jax.random.randint(streams_of[8], (WET_DEV * SHARDS,), 0, AROWS_DEV), jax.random.fold_in(streams_of[8], 1), 0, AROWS_DEV - 1).astype(jnp.int32)
    wet_dest_keys = jax.random.split(jax.random.fold_in(streams_of[9], 1), (WET_DEV * SHARDS) // WET_DEV)
    wet_dest_turns = jax.random.permutation(jax.random.fold_in(streams_of[9], 3), (WET_DEV * SHARDS) // WET_DEV)
    wet_dest = jax.vmap(lambda own, number: assign_block(jax.random.fold_in(streams_of[9], 2), own, number, WET_DEV, SHARDS, 1, CAP, 2))(wet_dest_keys, wet_dest_turns).reshape((WET_DEV * SHARDS, 1))
    coupling = noise(streams_of[10], (NS, NREC), (NS * SHARDS * CAP) ** -0.5, 0.001953125, ((0, 128),), jnp.float32)
    return dict(struct_basis=struct_basis, fluid_basis=fluid_basis, stiff_tiles=stiff_tiles, mass_tiles=mass_tiles, fluid_stiff_tiles=fluid_stiff_tiles, fluid_mass_tiles=fluid_mass_tiles, struct_cols=struct_cols, fluid_cols=fluid_cols, wet_rows=wet_rows, wet_dest=wet_dest, coupling=coupling)


exact_precision = lax.Precision.HIGHEST


def tile_product(tiles, columns, extended):
    blocks = extended.reshape(-1, TILE, R)
    picked = jnp.take(blocks, columns, axis=0)
    result = jnp.einsum("tbij,tbjr->tir", tiles, picked, precision=exact_precision)
    return result.reshape(-1, R)


def congruence(left_basis, image):
    return jnp.einsum("nr,ns->rs", left_basis, image, precision=exact_precision)


def slot_numbers(targets):
    shard_count = N_ROW * N_COL
    onehot = (targets[:, None] == jnp.arange(shard_count, dtype=jnp.int32)[None, :]).astype(jnp.int32)
    before = jnp.cumsum(onehot, axis=0) - onehot
    return jnp.sum(before * onehot, axis=1).astype(jnp.int32)


def extend(basis, device, height):
    shard_count = N_ROW * N_COL
    border = HALO * TILE
    total_rows = basis.shape[0]
    start = (device * height).astype(jnp.int32)
    own_block = lax.dynamic_slice_in_dim(basis, start, height, 0)
    lower = lax.dynamic_slice_in_dim(basis, jnp.maximum(start - border, 0).astype(jnp.int32), border, 0)
    upper = lax.dynamic_slice_in_dim(basis, jnp.minimum(start + height, total_rows - border).astype(jnp.int32), border, 0)
    lower = lower * (device > 0).astype(basis.dtype)
    upper = upper * (device < shard_count - 1).astype(basis.dtype)
    return own_block, jnp.concatenate([lower, own_block, upper], axis=0)


def reference(struct_basis, fluid_basis, stiff_tiles, mass_tiles, fluid_stiff_tiles, fluid_mass_tiles, struct_cols, fluid_cols, wet_rows, wet_dest, coupling):
    shard_count = N_ROW * N_COL
    struct_height = STILE_DEV * TILE
    fluid_height = ATILE_DEV * TILE
    slot_total = shard_count * CAP
    destination = wet_dest[:, 0].reshape(shard_count, WET_DEV)
    slot_index = lax.map(slot_numbers, destination)
    source = jnp.arange(shard_count, dtype=jnp.int32)[:, None]
    target = (source * CAP + slot_index).reshape(-1).astype(jnp.int32)
    flat_dest = destination.reshape(-1)
    global_rows = (source * fluid_height + wet_rows.reshape(shard_count, WET_DEV)).reshape(-1).astype(jnp.int32)
    wet_values = jnp.take(fluid_basis, global_rows, axis=0)

    def step(totals, device):
        def device_part(array, count):
            return lax.dynamic_slice_in_dim(array, (device * count).astype(jnp.int32), count, 0)

        own_struct, extended_struct = extend(struct_basis, device, struct_height)
        own_fluid, extended_fluid = extend(fluid_basis, device, fluid_height)
        stiff_part = congruence(own_struct, tile_product(device_part(stiff_tiles, STILE_DEV), device_part(struct_cols, STILE_DEV), extended_struct))
        mass_part = congruence(own_struct, tile_product(device_part(mass_tiles, STILE_DEV), device_part(struct_cols, STILE_DEV), extended_struct))
        fstiff_part = congruence(own_fluid, tile_product(device_part(fluid_stiff_tiles, ATILE_DEV), device_part(fluid_cols, ATILE_DEV), extended_fluid))
        fmass_part = congruence(own_fluid, tile_product(device_part(fluid_mass_tiles, ATILE_DEV), device_part(fluid_cols, ATILE_DEV), extended_fluid))
        places = jnp.where(flat_dest == device, target, slot_total).astype(jnp.int32)
        received = jnp.zeros((slot_total, R), fluid_basis.dtype).at[places].set(wet_values, mode="drop")
        projected = jnp.einsum("nr,nk->rk", own_struct, device_part(coupling, struct_height), precision=exact_precision)
        coupled_part = jnp.dot(projected, received, precision=exact_precision)
        updated = (totals[0] + stiff_part, totals[1] + mass_part, totals[2] + fstiff_part, totals[3] + fmass_part, totals[4] + coupled_part)
        return updated, None

    empty_sum = jnp.zeros((R, R), struct_basis.dtype)
    totals, unused = lax.scan(step, (empty_sum, empty_sum, empty_sum, empty_sum, empty_sum), jnp.arange(shard_count, dtype=jnp.int32))
    return (totals[0], totals[1], totals[2], totals[3], totals[4])
```

```python
import functools

import jax
import jax.numpy as jnp
from jax import lax
from jax.experimental import pallas as pl
from jax.experimental.pallas import tpu as pltpu
from jax.sharding import Mesh
from jax.sharding import PartitionSpec as P

R = 1024
TILE = 128
CAP = 2
F32 = jnp.float32
BF16 = jnp.bfloat16

AXES = ("zhi", "x", "core", "y", "zlo")
ROW = ("zhi", "x", "core")
COL = ("y", "zlo")
X, Y, Z = "x", "y", ("zhi", "zlo")
NX = 24
NY = 24
NZ = 16


VMEM = pl.BlockSpec(memory_space=pltpu.VMEM)
SMEM = pl.BlockSpec(memory_space=pltpu.SMEM)
PARAMS = pltpu.CompilerParams(vmem_limit_bytes=60 * 1024 * 1024)


def shape(*dims):
    return jax.ShapeDtypeStruct(dims, F32)


def parts(value):
    high = value.astype(BF16)
    low = (value - high.astype(F32)).astype(BF16)
    return high, low


def mul(a, b):
    return jnp.dot(a, b, preferred_element_type=F32)


def product(a, b):
    ah, al = a
    bh, bl = b
    return mul(ah, bh) + (mul(ah, bl) + mul(al, bh))


def shifted(value, axis, by):
    size = lax.axis_size(axis)
    return lax.ppermute(value, axis, [(i, (i + by) % size) for i in range(size)])


def from_behind(value, by):
    size = lax.axis_size(AXES)
    pairs = [(i, i + by) for i in range(size) if 0 <= i + by < size]
    return lax.ppermute(value, AXES, pairs)


def route_kernel(dest_col, dest_row, rows, fluid, out):
    n = dest_row.shape[1]
    earlier = lax.broadcasted_iota(jnp.int32, (n, n), 0) < lax.broadcasted_iota(jnp.int32, (n, n), 1)
    same = (dest_col[...] == dest_row[...]) & earlier
    slot = jnp.sum(jnp.where(same, 1.0, 0.0), axis=0, keepdims=True).astype(jnp.int32)
    target = dest_row[...] * CAP + slot
    q = out.shape[0]
    selector = jnp.where(lax.broadcasted_iota(jnp.int32, (q, n), 0) == target, 1.0, 0.0).astype(BF16)
    height = fluid.shape[0]
    picked = jnp.where(lax.broadcasted_iota(jnp.int32, (height, n), 0) == rows[...], 1.0, 0.0)
    chosen = lax.dot_general(
        selector, picked.astype(BF16), (((1,), (1,)), ((), ())), preferred_element_type=F32
    ).astype(BF16)
    value = fluid[...]
    high = value.astype(BF16)
    rest = value - high.astype(F32)
    mid = rest.astype(BF16)
    low = (rest - mid.astype(F32)).astype(BF16)
    out[...] = mul(chosen, high) + (mul(chosen, mid) + mul(chosen, low))


def turn_kernel(place, struct, fluid, own_s, send_s, own_f, send_f, held_s, held_f):
    core = place[3]
    held_s[...] = struct[...].T.reshape(held_s.shape)
    held_f[...] = fluid[...].T.reshape(held_f.shape)
    own_s[...] = held_s[:, core]
    send_s[...] = held_s[:, 1 - core]
    own_f[...] = held_f[:, core]
    send_f[...] = held_f[:, 1 - core]


def wet_kernel(coupling, received, out):
    out[...] = product(parts(coupling[...]), parts(received[...]))


def gathered(tiles, cols, total, at):
    total[:, at : at + TILE * tiles.shape[0]] = jnp.zeros(
        (total.shape[0], TILE * tiles.shape[0], TILE), F32
    )
    for i in range(tiles.shape[0]):
        rows = pl.ds(at + i * TILE, TILE)
        for k in range(tiles.shape[1]):
            c = cols[i, k]
            total[c, rows] = total[c, rows] + tiles[i, k]


def image(total, pieces):
    acc = None
    c = 0
    for piece in pieces:
        n = piece.shape[0] // TILE
        left = jnp.concatenate([total[c + i] for i in range(n)], axis=1) if n > 1 else total[c]
        term = product(parts(left), parts(piece))
        acc = term if acc is None else acc + term
        c += n
    return acc


def image_kernel(
    s_cols, f_cols, stiff, mass, fstiff, fmass, s_lo, s_own, s_hi, f_lo, f_own, f_hi, out_s, out_f, w_s, w_f
):
    gathered(stiff, s_cols, w_s, 0)
    gathered(mass, s_cols, w_s, 2 * TILE)
    gathered(fstiff, f_cols, w_f, 0)
    gathered(fmass, f_cols, w_f, TILE)
    out_f[...] = image(w_f, (f_lo[...], f_own[...], f_hi[...])).reshape(out_f.shape)
    out_s[...] = image(w_s, (s_lo[...], s_own[...], s_hi[...])).reshape(out_s.shape)


def reduced_kernel(place, ls0, ls1, lf0, lf1, is0, is1, ic0, ic1, if0, if1, *rest):
    outs, (sh, sl, fh, fl, held) = rest[:12], rest[12:]
    m = pl.program_id(0)
    half = R // 2

    @pl.when(m == 0)
    def _():
        left = jnp.concatenate([ls0[...].reshape(half, -1), ls1[...].reshape(half, -1)], axis=1)
        sh[...], sl[...] = parts(left)
        left = jnp.concatenate([lf0[...].reshape(half, -1), lf1[...].reshape(half, -1)], axis=1)
        fh[...], fl[...] = parts(left)

    def multiply(high, low, one, two):
        right = jnp.concatenate([one, two], axis=0)
        held[...] = product((high[...], low[...]), parts(right)).reshape(held.shape)

    @pl.when(m < 2)
    def _():
        multiply(sh, sl, is0[0], is1[0])

    @pl.when(m == 2)
    def _():
        multiply(sh, sl, ic0[...], ic1[...])

    @pl.when(m > 2)
    def _():
        multiply(fh, fl, if0[0], if1[0])

    for o in range(4):
        dx = lax.rem(place[0] + o, 4)
        dy = lax.rem(place[1] + o, 4)
        dz = lax.rem(place[2] + o, 4)
        zh, zl = dz // 2, lax.rem(dz, 2)
        for h in range(2):
            outs[o][0, h] = held[h * 4 + dx, 0:NX, :]
        outs[4 + o][0] = held[:, NX : NX + NY, pl.ds(pl.multiple_of(dy * 256, 256), 256)]
        for y in range(4):
            lanes = pl.ds(pl.multiple_of(y * 256 + zl * 128, 128), 128)
            outs[8 + o][0, :, :, y * 128 : (y + 1) * 128] = held[pl.ds(zh * 4, 4), NX + NY :, lanes]


def split_kernel(axis, place, a0, a1, a2, a3, o0, o1, o2, o3, held):
    held[...] = (a0[...] + a1[...]) + (a2[...] + a3[...])
    rank = len(held.shape)
    for o, out in enumerate((o0, o1, o2, o3)):
        d = lax.rem(place[{"x": 0, "y": 1, "z": 2}[axis]] + o, 4)
        if axis == "y":
            width = held.shape[-1] // 4
            lanes = pl.ds(pl.multiple_of(d * width, width), width)
            out[...] = held[..., lanes]
        elif axis == "x":
            out[...] = held[:, d]
        else:
            zh, zl = d // 2, lax.rem(d, 2)
            lanes = pl.ds(pl.multiple_of(zl * 128, 128), 128)
            if rank == 4 and held.shape[1] == 2:
                out[...] = held[:, zh, :, lanes]
            else:
                out[...] = held[:, pl.ds(zh * 4, 4), :, lanes]


def last_kernel(*refs):
    ins, outs = refs[:12], refs[12:]
    for m, out in enumerate(outs):
        for base, at, n in ((0, 0, NX), (4, NX, NY), (8, NX + NY, NZ)):
            a, b, c, d = ins[base : base + 4]
            out[at : at + n] = (a[m] + b[m]) + (c[m] + d[m])


def call(kernel, out, count, smem=0, scratch=(), flops=0, moved=0):
    return pl.pallas_call(
        kernel,
        out_shape=out,
        in_specs=[SMEM] * smem + [VMEM] * (count - smem),
        out_specs=jax.tree.map(lambda _: VMEM, out),
        scratch_shapes=list(scratch),
        compiler_params=PARAMS,
        cost_estimate=pl.CostEstimate(flops=flops, bytes_accessed=moved, transcendentals=0),
    )


def exchanged(slots, axis):
    return [slots[0]] + [shifted(slots[o], axis, o) for o in range(1, 4)]


def split(place, arrived, axis, out_shape):
    held = arrived[0].shape
    size = 4 * arrived[0].size
    return call(
        functools.partial(split_kernel, axis),
        [shape(*out_shape)] * 4,
        5,
        smem=1,
        scratch=[pltpu.VMEM(held, F32)],
        flops=3 * arrived[0].size,
        moved=5 * size,
    )(place, *arrived)


def on_device(
    struct_basis,
    fluid_basis,
    stiff_tiles,
    mass_tiles,
    fluid_stiff_tiles,
    fluid_mass_tiles,
    struct_cols,
    fluid_cols,
    wet_rows,
    wet_dest,
    coupling,
):
    place = jnp.stack([lax.axis_index(X), lax.axis_index(Y), lax.axis_index(Z), lax.axis_index("core")]).astype(
        jnp.int32
    )
    below_s = from_behind(struct_basis[-TILE:], 1)
    above_s = from_behind(struct_basis[:TILE], -1)
    below_f = from_behind(fluid_basis, 1)
    above_f = from_behind(fluid_basis, -1)

    outgoing = call(route_kernel, shape(256, R), 4, flops=2 * 3 * 256 * 128 * R, moved=2**21)(
        wet_dest, wet_dest.reshape(1, -1), wet_rows.reshape(1, -1), fluid_basis
    )
    received = lax.all_to_all(outgoing, AXES, split_axis=0, concat_axis=0, tiled=True)

    own_s, send_s, own_f, send_f = call(
        turn_kernel,
        [shape(8, 64, 256)] * 2 + [shape(8, 64, 128)] * 2,
        3,
        smem=1,
        scratch=[pltpu.VMEM((8, 2, 64, 256), F32), pltpu.VMEM((8, 2, 64, 128), F32)],
        flops=2**20,
        moved=3 * 2**20,
    )(place, struct_basis, fluid_basis)
    left_s = shifted(send_s, "core", 1)
    left_f = shifted(send_f, "core", 1)

    image_c = call(wet_kernel, shape(256, R), 2, flops=6 * 256 * 256 * R, moved=2**21)(coupling, received)
    other_c = shifted(image_c, "core", 1)

    image_s, image_f = call(
        image_kernel,
        [shape(2, 256, R), shape(2, 128, R)],
        12,
        smem=2,
        scratch=[pltpu.VMEM((4, 512, TILE), F32), pltpu.VMEM((3, 256, TILE), F32)],
        flops=6 * 512 * 512 * R,
        moved=8 * 2**20,
    )(
        struct_cols,
        fluid_cols,
        stiff_tiles,
        mass_tiles,
        fluid_stiff_tiles,
        fluid_mass_tiles,
        below_s,
        struct_basis,
        above_s,
        below_f,
        fluid_basis,
        above_f,
    )
    other_s = shifted(image_s, "core", 1)
    other_f = shifted(image_f, "core", 1)

    sblock = pl.BlockSpec((1, 256, R), lambda m: (jnp.minimum(m, 1), 0, 0))
    fblock = pl.BlockSpec((1, 128, R), lambda m: (jnp.maximum(m - 3, 0), 0, 0))
    slots = pl.pallas_call(
        reduced_kernel,
        grid=(5,),
        out_shape=[shape(5, 2, NX, R)] * 4 + [shape(5, 8, NY, 256)] * 4 + [shape(5, 4, NZ, 512)] * 4,
        in_specs=[SMEM, VMEM, VMEM, VMEM, VMEM, sblock, sblock, VMEM, VMEM, fblock, fblock],
        out_specs=[pl.BlockSpec((1, 2, NX, R), lambda m: (m, 0, 0, 0))] * 4
        + [pl.BlockSpec((1, 8, NY, 256), lambda m: (m, 0, 0, 0))] * 4
        + [pl.BlockSpec((1, 4, NZ, 512), lambda m: (m, 0, 0, 0))] * 4,
        scratch_shapes=[
            pltpu.VMEM((512, 512), BF16),
            pltpu.VMEM((512, 512), BF16),
            pltpu.VMEM((512, 256), BF16),
            pltpu.VMEM((512, 256), BF16),
            pltpu.VMEM((8, 64, R), F32),
        ],
        compiler_params=PARAMS,
        cost_estimate=pl.CostEstimate(flops=24 * 512 * 512 * R, bytes_accessed=20 * 2**20, transcendentals=0),
    )(place, own_s, left_s, own_f, left_f, image_s, other_s, image_c, other_c, image_f, other_f)

    fx = exchanged(slots[0:4], X)
    fy = exchanged(slots[4:8], Y)
    fz = exchanged(slots[8:12], Z)
    gx = exchanged(split(place, fx, "y", (5, 2, NX, 256)), Y)
    gy = exchanged(split(place, fy, "z", (5, 4, NY, 128)), Z)
    gz = exchanged(split(place, fz, "x", (5, NZ, 512)), X)
    hx = exchanged(split(place, gx, "z", (5, NX, 128)), Z)
    hy = exchanged(split(place, gy, "x", (5, NY, 128)), X)
    hz = exchanged(split(place, gz, "y", (5, NZ, 128)), Y)
    results = call(last_kernel, [shape(64, 128)] * 5, 12, flops=2**18, moved=2**20)(*hx, *hy, *hz)
    stiff, mass, wet, fstiff, fmass = results
    return stiff, mass, fstiff, fmass, wet


def solution(mesh):
    fine = Mesh(mesh.devices.reshape(2, 4, 2, 4, 2), AXES)
    return jax.shard_map(
        on_device,
        mesh=fine,
        in_specs=(
            P(AXES, None),
            P(AXES, None),
            P(AXES, None, None, None),
            P(AXES, None, None, None),
            P(AXES, None, None, None),
            P(AXES, None, None, None),
            P(AXES, None),
            P(AXES, None),
            P(AXES),
            P(AXES, None),
            P(AXES, None),
        ),
        out_specs=(P(ROW, COL),) * 5,
        check_vma=False,
    )
```

```python
import functools

import jax
import jax.numpy as jnp
from jax import lax
from jax.experimental import pallas as pl
from jax.experimental.pallas import tpu as pltpu
from jax.sharding import Mesh
from jax.sharding import PartitionSpec as P


R = 1024
TILE = 128
CAP = 2
F32 = jnp.float32
BF16 = jnp.bfloat16

AXES = ("zhi", "x", "core", "y", "zlo")
ROW = ("zhi", "x", "core")
COL = ("y", "zlo")
X, Y, Z = "x", "y", ("zhi", "zlo")
HALF = 32


VMEM = pl.BlockSpec(memory_space=pltpu.VMEM)
SMEM = pl.BlockSpec(memory_space=pltpu.SMEM)
ANY = pl.BlockSpec(memory_space=pl.ANY)
PARAMS = pltpu.CompilerParams(vmem_limit_bytes=60 * 1024 * 1024)


def shape(*dims):
    return jax.ShapeDtypeStruct(dims, F32)


def parts(value):
    high = value.astype(BF16)
    low = (value - high.astype(F32)).astype(BF16)
    return high, low


def mul(a, b):
    return jnp.dot(a, b, preferred_element_type=F32)


def product(a, b):
    ah, al = a
    bh, bl = b
    return mul(ah, bh) + (mul(ah, bl) + mul(al, bh))


def shifted(value, axis, by):
    size = lax.axis_size(axis)
    return lax.ppermute(value, axis, [(i, (i + by) % size) for i in range(size)])


def from_behind(value, by):
    size = lax.axis_size(AXES)
    pairs = [(i, i + by) for i in range(size) if 0 <= i + by < size]
    return lax.ppermute(value, AXES, pairs)


def route_kernel(dest_col, dest_row, rows, fluid, out):
    n = dest_row.shape[1]
    earlier = lax.broadcasted_iota(jnp.int32, (n, n), 0) < lax.broadcasted_iota(jnp.int32, (n, n), 1)
    same = (dest_col[...] == dest_row[...]) & earlier
    slot = jnp.sum(jnp.where(same, 1.0, 0.0), axis=0, keepdims=True).astype(jnp.int32)
    target = dest_row[...] * CAP + slot
    q = out.shape[0]
    selector = jnp.where(lax.broadcasted_iota(jnp.int32, (q, n), 0) == target, 1.0, 0.0).astype(BF16)
    height = fluid.shape[0]
    picked = jnp.where(lax.broadcasted_iota(jnp.int32, (height, n), 0) == rows[...], 1.0, 0.0)
    chosen = lax.dot_general(
        selector, picked.astype(BF16), (((1,), (1,)), ((), ())), preferred_element_type=F32
    ).astype(BF16)
    value = fluid[...]
    high = value.astype(BF16)
    rest = value - high.astype(F32)
    mid = rest.astype(BF16)
    low = (rest - mid.astype(F32)).astype(BF16)
    out[...] = mul(chosen, high) + (mul(chosen, mid) + mul(chosen, low))


def turn_kernel(place, struct, fluid, own_s, send_s, own_f, send_f, held_s, held_f):
    core = place[3]
    held_s[...] = struct[...].T.reshape(held_s.shape)
    held_f[...] = fluid[...].T.reshape(held_f.shape)
    own_s[...] = held_s[:, core]
    send_s[...] = held_s[:, 1 - core]
    own_f[...] = held_f[:, core]
    send_f[...] = held_f[:, 1 - core]


def wet_kernel(coupling, received, out):
    out[...] = product(parts(coupling[...]), parts(received[...]))


def gathered(tiles, cols, total, at):
    total[:, at : at + TILE * tiles.shape[0]] = jnp.zeros(
        (total.shape[0], TILE * tiles.shape[0], TILE), F32
    )
    for i in range(tiles.shape[0]):
        rows = pl.ds(at + i * TILE, TILE)
        for k in range(tiles.shape[1]):
            c = cols[i, k]
            total[c, rows] = total[c, rows] + tiles[i, k]


def image(total, pieces):
    acc = None
    c = 0
    for piece in pieces:
        n = piece.shape[0] // TILE
        left = jnp.concatenate([total[c + i] for i in range(n)], axis=1) if n > 1 else total[c]
        term = product(parts(left), parts(piece))
        acc = term if acc is None else acc + term
        c += n
    return acc


def fluid_kernel(cols, stiff, mass, lo, own, hi, after_a, after_b, out, total):
    gathered(stiff, cols, total, 0)
    gathered(mass, cols, total, TILE)
    out[...] = image(total, (lo[...], own[...], hi[...])).reshape(out.shape)


def struct_kernel(cols, stiff, mass, lo, own, hi, after, out, total):
    gathered(stiff, cols, total, 0)
    gathered(mass, cols, total, 2 * TILE)
    out[...] = image(total, (lo[...], own[...], hi[...])).reshape(out.shape)


def joined(one, two):
    return jnp.concatenate([one[...].reshape(R // 2, -1), two[...].reshape(R // 2, -1)], axis=1)


def multiply(held, left, one, two):
    right = jnp.concatenate([one, two], axis=0)
    held[...] = product((left[0][...], left[1][...]), parts(right)).reshape(held.shape)


def send_off(place, held, outs):
    for o in range(4):
        dx = lax.rem(place[0] + o, 4)
        dy = lax.rem(place[1] + o, 4)
        for h in range(2):
            outs[o][0, h] = held[h * 4 + dx, 0:HALF, :]
        outs[4 + o][0] = held[:, HALF:, pl.ds(pl.multiple_of(dy * 256, 256), 256)]


def first_kernel(place, ls0, ls1, lf0, lf1, ic0, ic1, if0, if1, *rest):
    outs, (sh, sl, fh, fl, held) = rest[:8], rest[8:]
    m = pl.program_id(0)

    @pl.when(m == 0)
    def _():
        sh[...], sl[...] = parts(joined(ls0, ls1))
        fh[...], fl[...] = parts(joined(lf0, lf1))
        multiply(held, (sh, sl), ic0[...], ic1[...])

    @pl.when(m > 0)
    def _():
        multiply(held, (fh, fl), if0[0], if1[0])

    send_off(place, held, outs)


def second_kernel(place, ls0, ls1, is0, is1, *rest):
    outs, (sh, sl, held) = rest[:8], rest[8:]

    @pl.when(pl.program_id(0) == 0)
    def _():
        sh[...], sl[...] = parts(joined(ls0, ls1))

    multiply(held, (sh, sl), is0[0], is1[0])
    send_off(place, held, outs)


def split_kernel(axis, place, a0, a1, a2, a3, b0, b1, b2, b3, o0, o1, o2, o3, held):
    n = a0.shape[0]
    held[:n] = (a0[...] + a1[...]) + (a2[...] + a3[...])
    held[n:] = (b0[...] + b1[...]) + (b2[...] + b3[...])
    for o, out in enumerate((o0, o1, o2, o3)):
        d = lax.rem(place[axis] + o, 4)
        if axis == 1:
            out[...] = held[..., pl.ds(pl.multiple_of(d * 256, 256), 256)]
        else:
            for h in range(2):
                out[:, h] = held[:, h * 4 + d]


def spread_kernel(x0, x1, x2, x3, y0, y1, y2, y3, out):
    for h in range(2):
        top = (x0[:, h] + x1[:, h]) + (x2[:, h] + x3[:, h])
        low = (y0[:, h] + y1[:, h]) + (y2[:, h] + y3[:, h])
        for l in range(2):
            lanes = slice(l * 128, (l + 1) * 128)
            out[h * 2 + l, :, 0:HALF] = top[..., lanes]
            out[h * 2 + l, :, HALF:] = low[..., lanes]


def last_kernel(arrived, *outs):
    for m, out in enumerate(outs):
        out[...] = (arrived[0, m] + arrived[1, m]) + (arrived[2, m] + arrived[3, m])


def call(kernel, out, count, smem=0, anywhere=0, scratch=(), flops=0, moved=0):
    run = pl.pallas_call(
        kernel,
        out_shape=out,
        in_specs=[SMEM] * smem + [VMEM] * (count - smem - anywhere) + [ANY] * anywhere,
        out_specs=jax.tree.map(lambda _: VMEM, out),
        scratch_shapes=list(scratch),
        compiler_params=PARAMS,
        cost_estimate=pl.CostEstimate(flops=flops, bytes_accessed=moved, transcendentals=0),
    )
    return run


def exchanged(slots, axis):
    return [slots[0]] + [shifted(slots[o], axis, o) for o in range(1, 4)]


def split(place, one, two, axis):
    dims = (one[0].shape[0] + two[0].shape[0],) + one[0].shape[1:]
    size = one[0].size + two[0].size
    return call(
        functools.partial(split_kernel, axis),
        [shape(5, 2, HALF, 256)] * 4,
        9,
        smem=1,
        scratch=[pltpu.VMEM(dims, F32)],
        flops=3 * size,
        moved=20 * size,
    )(place, *one, *two)


def partial_sums(kernel, count, place, lefts, steps, operands, specs, scratch):
    run = pl.pallas_call(
        kernel,
        grid=(count,),
        out_shape=[shape(count, 2, HALF, R)] * 4 + [shape(count, 8, HALF, 256)] * 4,
        in_specs=[SMEM] + [VMEM] * len(lefts) + specs,
        out_specs=[pl.BlockSpec((1, 2, HALF, R), lambda m: (m, 0, 0, 0))] * 4
        + [pl.BlockSpec((1, 8, HALF, 256), lambda m: (m, 0, 0, 0))] * 4,
        scratch_shapes=scratch + [pltpu.VMEM((8, 64, R), F32)],
        compiler_params=PARAMS,
        cost_estimate=pl.CostEstimate(
            flops=6 * steps * 512 * 256 * R, bytes_accessed=4 * count * 2**20, transcendentals=0
        ),
    )
    return run(place, *lefts, *operands)


def compute(
    struct_basis,
    fluid_basis,
    stiff_tiles,
    mass_tiles,
    fluid_stiff_tiles,
    fluid_mass_tiles,
    struct_cols,
    fluid_cols,
    wet_rows,
    wet_dest,
    coupling,
):
    place = jnp.stack([lax.axis_index(X), lax.axis_index(Y), lax.axis_index(Z), lax.axis_index("core")]).astype(
        jnp.int32
    )
    below_s = from_behind(struct_basis[-TILE:], 1)
    above_s = from_behind(struct_basis[:TILE], -1)
    below_f = from_behind(fluid_basis, 1)
    above_f = from_behind(fluid_basis, -1)

    outgoing = call(route_kernel, shape(256, R), 4, flops=2 * 3 * 256 * 128 * R, moved=2**21)(
        wet_dest, wet_dest.reshape(1, -1), wet_rows.reshape(1, -1), fluid_basis
    )
    received = lax.all_to_all(outgoing, AXES, split_axis=0, concat_axis=0, tiled=True)

    own_s, send_s, own_f, send_f = call(
        turn_kernel,
        [shape(8, 64, 256)] * 2 + [shape(8, 64, 128)] * 2,
        3,
        smem=1,
        scratch=[pltpu.VMEM((8, 2, 64, 256), F32), pltpu.VMEM((8, 2, 64, 128), F32)],
        flops=2**20,
        moved=3 * 2**20,
    )(place, struct_basis, fluid_basis)
    left_s = shifted(send_s, "core", 1)
    left_f = shifted(send_f, "core", 1)

    image_c = call(wet_kernel, shape(256, R), 2, flops=6 * 256 * 256 * R, moved=2**21)(coupling, received)
    other_c = shifted(image_c, "core", 1)

    image_f = call(
        fluid_kernel,
        shape(2, 128, R),
        8,
        smem=1,
        anywhere=2,
        scratch=[pltpu.VMEM((3, 256, TILE), F32)],
        flops=6 * 256 * 384 * R,
        moved=3 * 2**20,
    )(fluid_cols, fluid_stiff_tiles, fluid_mass_tiles, below_f, fluid_basis, above_f, image_c, own_s)
    other_f = shifted(image_f, "core", 1)

    fblock = pl.BlockSpec((1, 128, R), lambda m: (jnp.maximum(m - 1, 0), 0, 0))
    slim = [pltpu.VMEM((512, 512), BF16)] * 2
    first = partial_sums(
        first_kernel,
        3,
        place,
        (own_s, left_s, own_f, left_f, image_c, other_c),
        4,
        (image_f, other_f),
        [fblock, fblock],
        slim + [pltpu.VMEM((512, 256), BF16)] * 2,
    )
    first_x = exchanged(first[0:4], X)
    first_y = exchanged(first[4:8], Y)

    image_s = call(
        struct_kernel,
        shape(2, 256, R),
        7,
        smem=1,
        anywhere=1,
        scratch=[pltpu.VMEM((4, 512, TILE), F32)],
        flops=6 * 512 * 512 * R,
        moved=5 * 2**20,
    )(struct_cols, stiff_tiles, mass_tiles, below_s, struct_basis, above_s, first[0])
    other_s = shifted(image_s, "core", 1)

    sblock = pl.BlockSpec((1, 256, R), lambda m: (m, 0, 0))
    second = partial_sums(second_kernel, 2, place, (own_s, left_s), 4, (image_s, other_s), [sblock, sblock], slim)
    second_x = exchanged(second[0:4], X)
    second_y = exchanged(second[4:8], Y)

    then_y = exchanged(split(place, first_x, second_x, 1), Y)
    then_x = exchanged(split(place, first_y, second_y, 0), X)
    blocks = call(spread_kernel, shape(4, 5, 64, 128), 8, flops=2**20, moved=2**22)(*then_y, *then_x)
    arrived = lax.all_to_all(blocks, Z, split_axis=0, concat_axis=0, tiled=True)
    wet, fstiff, fmass, stiff, mass = call(last_kernel, [shape(64, 128)] * 5, 1, flops=2**18, moved=2**20)(arrived)
    return stiff, mass, fstiff, fmass, wet


def solution(mesh):
    fine = Mesh(mesh.devices.reshape(2, 4, 2, 4, 2), AXES)
    return jax.shard_map(
        compute,
        mesh=fine,
        in_specs=(
            P(AXES, None),
            P(AXES, None),
            P(AXES, None, None, None),
            P(AXES, None, None, None),
            P(AXES, None, None, None),
            P(AXES, None, None, None),
            P(AXES, None),
            P(AXES, None),
            P(AXES),
            P(AXES, None),
            P(AXES, None),
        ),
        out_specs=(P(ROW, COL),) * 5,
        check_vma=False,
    )
```

```python
import functools

import jax
import jax.numpy as jnp
from jax import lax
from jax.experimental import pallas as pl
from jax.experimental.pallas import tpu as pltpu
from jax.sharding import Mesh
from jax.sharding import PartitionSpec as P


R = 1024
TILE = 128
CAP = 2
F32 = jnp.float32
BF16 = jnp.bfloat16

AXES = ("zhi", "x", "core", "y", "zlo")
ROW = ("zhi", "x", "core")
COL = ("y", "zlo")
X, Y, Z = "x", "y", ("zhi", "zlo")
HALF = 32


VMEM = pl.BlockSpec(memory_space=pltpu.VMEM)
SMEM = pl.BlockSpec(memory_space=pltpu.SMEM)
ANY = pl.BlockSpec(memory_space=pl.ANY)
PARAMS = pltpu.CompilerParams(vmem_limit_bytes=60 * 1024 * 1024)


def shape(*dims):
    return jax.ShapeDtypeStruct(dims, F32)


def parts(value):
    high = value.astype(BF16)
    low = (value - high.astype(F32)).astype(BF16)
    return high, low


def mul(a, b):
    return jnp.dot(a, b, preferred_element_type=F32)


def product(a, b):
    ah, al = a
    bh, bl = b
    return mul(ah, bh) + (mul(ah, bl) + mul(al, bh))


def shifted(value, axis, by):
    size = lax.axis_size(axis)
    return lax.ppermute(value, axis, [(i, (i + by) % size) for i in range(size)])


def from_behind(value, by):
    size = lax.axis_size(AXES)
    pairs = [(i, i + by) for i in range(size) if 0 <= i + by < size]
    return lax.ppermute(value, AXES, pairs)


def route_kernel(dest_col, dest_row, rows, fluid, out):
    n = dest_row.shape[1]
    earlier = lax.broadcasted_iota(jnp.int32, (n, n), 0) < lax.broadcasted_iota(jnp.int32, (n, n), 1)
    same = (dest_col[...] == dest_row[...]) & earlier
    slot = jnp.sum(jnp.where(same, 1.0, 0.0), axis=0, keepdims=True).astype(jnp.int32)
    target = dest_row[...] * CAP + slot
    q = out.shape[0]
    selector = jnp.where(lax.broadcasted_iota(jnp.int32, (q, n), 0) == target, 1.0, 0.0).astype(BF16)
    height = fluid.shape[0]
    picked = jnp.where(lax.broadcasted_iota(jnp.int32, (height, n), 0) == rows[...], 1.0, 0.0)
    chosen = lax.dot_general(
        selector, picked.astype(BF16), (((1,), (1,)), ((), ())), preferred_element_type=F32
    ).astype(BF16)
    value = fluid[...]
    high = value.astype(BF16)
    rest = value - high.astype(F32)
    mid = rest.astype(BF16)
    low = (rest - mid.astype(F32)).astype(BF16)
    out[...] = mul(chosen, high) + (mul(chosen, mid) + mul(chosen, low))


def turn_kernel(place, struct, fluid, own_s, send_s, own_f, send_f, held_s, held_f):
    core = place[3]
    held_s[...] = struct[...].T.reshape(held_s.shape)
    held_f[...] = fluid[...].T.reshape(held_f.shape)
    own_s[...] = held_s[:, core]
    send_s[...] = held_s[:, 1 - core]
    own_f[...] = held_f[:, core]
    send_f[...] = held_f[:, 1 - core]


def wet_kernel(coupling, received, out):
    out[...] = product(parts(coupling[...]), parts(received[...]))


def gathered(tiles, cols, total, at):
    total[:, at : at + TILE * tiles.shape[0]] = jnp.zeros(
        (total.shape[0], TILE * tiles.shape[0], TILE), F32
    )
    for i in range(tiles.shape[0]):
        rows = pl.ds(at + i * TILE, TILE)
        for k in range(tiles.shape[1]):
            c = cols[i, k]
            total[c, rows] = total[c, rows] + tiles[i, k]


def image(total, pieces):
    acc = None
    c = 0
    for piece in pieces:
        n = piece.shape[0] // TILE
        left = jnp.concatenate([total[c + i] for i in range(n)], axis=1) if n > 1 else total[c]
        term = product(parts(left), parts(piece))
        acc = term if acc is None else acc + term
        c += n
    return acc


def fluid_kernel(cols, stiff, mass, lo, own, hi, after, out, total):
    gathered(stiff, cols, total, 0)
    gathered(mass, cols, total, TILE)
    out[...] = image(total, (lo[...], own[...], hi[...])).reshape(out.shape)


def struct_kernel(cols, stiff, mass, lo, own, hi, after, out, total):
    gathered(stiff, cols, total, 0)
    gathered(mass, cols, total, 2 * TILE)
    out[...] = image(total, (lo[...], own[...], hi[...])).reshape(out.shape)


def joined(one, two):
    return jnp.concatenate([one[...].reshape(R // 2, -1), two[...].reshape(R // 2, -1)], axis=1)


def multiply(held, left, one, two):
    right = jnp.concatenate([one, two], axis=0)
    held[...] = product((left[0][...], left[1][...]), parts(right)).reshape(held.shape)


def send_off(place, held, outs):
    for o in range(4):
        dx = lax.rem(place[0] + o, 4)
        dy = lax.rem(place[1] + o, 4)
        for h in range(2):
            outs[o][0, h] = held[h * 4 + dx, 0:HALF, :]
        outs[4 + o][0] = held[:, HALF:, pl.ds(pl.multiple_of(dy * 256, 256), 256)]


def first_kernel(place, ls0, ls1, lf0, lf1, ic0, ic1, if0, if1, *rest):
    outs, (sh, sl, fh, fl, held) = rest[:8], rest[8:]
    m = pl.program_id(0)

    @pl.when(m == 0)
    def _():
        sh[...], sl[...] = parts(joined(ls0, ls1))
        fh[...], fl[...] = parts(joined(lf0, lf1))
        multiply(held, (sh, sl), ic0[...], ic1[...])

    @pl.when(m > 0)
    def _():
        multiply(held, (fh, fl), if0[0], if1[0])

    send_off(place, held, outs)


def second_kernel(place, ls0, ls1, is0, is1, *rest):
    outs, (sh, sl, held) = rest[:8], rest[8:]

    @pl.when(pl.program_id(0) == 0)
    def _():
        sh[...], sl[...] = parts(joined(ls0, ls1))

    multiply(held, (sh, sl), is0[0], is1[0])
    send_off(place, held, outs)


def split_kernel(axis, place, a0, a1, a2, a3, o0, o1, o2, o3, held):
    held[...] = (a0[...] + a1[...]) + (a2[...] + a3[...])
    for o, out in enumerate((o0, o1, o2, o3)):
        d = lax.rem(place[axis] + o, 4)
        if axis == 1:
            out[...] = held[..., pl.ds(pl.multiple_of(d * 256, 256), 256)]
        else:
            for h in range(2):
                out[:, h] = held[:, h * 4 + d]


def spread_kernel(*refs):
    ins, out = refs[:16], refs[16]
    at = 0
    for group in range(2):
        x, y = ins[group * 8 : group * 8 + 4], ins[group * 8 + 4 : group * 8 + 8]
        n = x[0].shape[0]
        for h in range(2):
            top = (x[0][:, h] + x[1][:, h]) + (x[2][:, h] + x[3][:, h])
            low = (y[0][:, h] + y[1][:, h]) + (y[2][:, h] + y[3][:, h])
            for l in range(2):
                lanes = slice(l * 128, (l + 1) * 128)
                out[h * 2 + l, at : at + n, 0:HALF] = top[..., lanes]
                out[h * 2 + l, at : at + n, HALF:] = low[..., lanes]
        at += n


def last_kernel(arrived, *outs):
    for m, out in enumerate(outs):
        out[...] = (arrived[0, m] + arrived[1, m]) + (arrived[2, m] + arrived[3, m])


def call(kernel, out, count, smem=0, anywhere=0, scratch=(), flops=0, moved=0):
    run = pl.pallas_call(
        kernel,
        out_shape=out,
        in_specs=[SMEM] * smem + [VMEM] * (count - smem - anywhere) + [ANY] * anywhere,
        out_specs=jax.tree.map(lambda _: VMEM, out),
        scratch_shapes=list(scratch),
        compiler_params=PARAMS,
        cost_estimate=pl.CostEstimate(flops=flops, bytes_accessed=moved, transcendentals=0),
    )
    return run


def exchanged(slots, axis):
    return [slots[0]] + [shifted(slots[o], axis, o) for o in range(1, 4)]


def split(place, arrived, axis):
    count = arrived[0].shape[0]
    size = arrived[0].size
    return call(
        functools.partial(split_kernel, axis),
        [shape(count, 2, HALF, 256)] * 4,
        5,
        smem=1,
        scratch=[pltpu.VMEM(arrived[0].shape, F32)],
        flops=3 * size,
        moved=20 * size,
    )(place, *arrived)


def partial_sums(kernel, count, place, lefts, steps, operands, specs, scratch):
    run = pl.pallas_call(
        kernel,
        grid=(count,),
        out_shape=[shape(count, 2, HALF, R)] * 4 + [shape(count, 8, HALF, 256)] * 4,
        in_specs=[SMEM] + [VMEM] * len(lefts) + specs,
        out_specs=[pl.BlockSpec((1, 2, HALF, R), lambda m: (m, 0, 0, 0))] * 4
        + [pl.BlockSpec((1, 8, HALF, 256), lambda m: (m, 0, 0, 0))] * 4,
        scratch_shapes=scratch + [pltpu.VMEM((8, 64, R), F32)],
        compiler_params=PARAMS,
        cost_estimate=pl.CostEstimate(
            flops=6 * steps * 512 * 256 * R, bytes_accessed=4 * count * 2**20, transcendentals=0
        ),
    )
    return run(place, *lefts, *operands)


def compute(
    struct_basis,
    fluid_basis,
    stiff_tiles,
    mass_tiles,
    fluid_stiff_tiles,
    fluid_mass_tiles,
    struct_cols,
    fluid_cols,
    wet_rows,
    wet_dest,
    coupling,
):
    place = jnp.stack([lax.axis_index(X), lax.axis_index(Y), lax.axis_index(Z), lax.axis_index("core")]).astype(
        jnp.int32
    )
    below_s = from_behind(struct_basis[-TILE:], 1)
    above_s = from_behind(struct_basis[:TILE], -1)
    below_f = from_behind(fluid_basis, 1)
    above_f = from_behind(fluid_basis, -1)

    outgoing = call(route_kernel, shape(256, R), 4, flops=2 * 3 * 256 * 128 * R, moved=2**21)(
        wet_dest, wet_dest.reshape(1, -1), wet_rows.reshape(1, -1), fluid_basis
    )
    received = lax.all_to_all(outgoing, AXES, split_axis=0, concat_axis=0, tiled=True)

    own_s, send_s, own_f, send_f = call(
        turn_kernel,
        [shape(8, 64, 256)] * 2 + [shape(8, 64, 128)] * 2,
        3,
        smem=1,
        scratch=[pltpu.VMEM((8, 2, 64, 256), F32), pltpu.VMEM((8, 2, 64, 128), F32)],
        flops=2**20,
        moved=3 * 2**20,
    )(place, struct_basis, fluid_basis)
    left_s = shifted(send_s, "core", 1)
    left_f = shifted(send_f, "core", 1)

    image_c = call(wet_kernel, shape(256, R), 2, flops=6 * 256 * 256 * R, moved=2**21)(coupling, received)
    other_c = shifted(image_c, "core", 1)

    image_f = call(
        fluid_kernel,
        shape(2, 128, R),
        7,
        smem=1,
        anywhere=1,
        scratch=[pltpu.VMEM((3, 256, TILE), F32)],
        flops=6 * 256 * 384 * R,
        moved=3 * 2**20,
    )(fluid_cols, fluid_stiff_tiles, fluid_mass_tiles, below_f, fluid_basis, above_f, own_s)
    other_f = shifted(image_f, "core", 1)

    fblock = pl.BlockSpec((1, 128, R), lambda m: (jnp.maximum(m - 1, 0), 0, 0))
    slim = [pltpu.VMEM((512, 512), BF16)] * 2
    first = partial_sums(
        first_kernel,
        3,
        place,
        (own_s, left_s, own_f, left_f, image_c, other_c),
        4,
        (image_f, other_f),
        [fblock, fblock],
        slim + [pltpu.VMEM((512, 256), BF16)] * 2,
    )
    first_x = exchanged(first[0:4], X)
    first_y = exchanged(first[4:8], Y)

    image_s = call(
        struct_kernel,
        shape(2, 256, R),
        7,
        smem=1,
        anywhere=1,
        scratch=[pltpu.VMEM((4, 512, TILE), F32)],
        flops=6 * 512 * 512 * R,
        moved=5 * 2**20,
    )(struct_cols, stiff_tiles, mass_tiles, below_s, struct_basis, above_s, first[0])
    other_s = shifted(image_s, "core", 1)

    sblock = pl.BlockSpec((1, 256, R), lambda m: (m, 0, 0))
    second = partial_sums(second_kernel, 2, place, (own_s, left_s), 4, (image_s, other_s), [sblock, sblock], slim)
    second_x = exchanged(second[0:4], X)
    second_y = exchanged(second[4:8], Y)

    first_xy = exchanged(split(place, first_x, 1), Y)
    first_yx = exchanged(split(place, first_y, 0), X)
    second_xy = exchanged(split(place, second_x, 1), Y)
    second_yx = exchanged(split(place, second_y, 0), X)
    blocks = call(spread_kernel, shape(4, 5, 64, 128), 16, flops=2**20, moved=2**22)(
        *first_xy, *first_yx, *second_xy, *second_yx
    )
    arrived = lax.all_to_all(blocks, Z, split_axis=0, concat_axis=0, tiled=True)
    wet, fstiff, fmass, stiff, mass = call(last_kernel, [shape(64, 128)] * 5, 1, flops=2**18, moved=2**20)(arrived)
    return stiff, mass, fstiff, fmass, wet


def solution(mesh):
    fine = Mesh(mesh.devices.reshape(2, 4, 2, 4, 2), AXES)
    return jax.shard_map(
        compute,
        mesh=fine,
        in_specs=(
            P(AXES, None),
            P(AXES, None),
            P(AXES, None, None, None),
            P(AXES, None, None, None),
            P(AXES, None, None, None),
            P(AXES, None, None, None),
            P(AXES, None),
            P(AXES, None),
            P(AXES),
            P(AXES, None),
            P(AXES, None),
        ),
        out_specs=(P(ROW, COL),) * 5,
        check_vma=False,
    )
```

```python
import functools

import jax
import jax.numpy as jnp
from jax import lax
from jax.experimental import pallas as pl
from jax.experimental.pallas import tpu as pltpu
from jax.sharding import Mesh
from jax.sharding import PartitionSpec as P


R = 1024
TILE = 128
CAP = 2
F32 = jnp.float32
BF16 = jnp.bfloat16

AXES = ("zhi", "x", "core", "y", "zlo")
ROW = ("zhi", "x", "core")
COL = ("y", "zlo")
X, Y, Z = "x", "y", ("zhi", "zlo")
HALF = 32


VMEM = pl.BlockSpec(memory_space=pltpu.VMEM)
SMEM = pl.BlockSpec(memory_space=pltpu.SMEM)
ANY = pl.BlockSpec(memory_space=pl.ANY)
PARAMS = pltpu.CompilerParams(vmem_limit_bytes=60 * 1024 * 1024)


def shape(*dims):
    return jax.ShapeDtypeStruct(dims, F32)


def parts(value):
    high = value.astype(BF16)
    low = (value - high.astype(F32)).astype(BF16)
    return high, low


def mul(a, b):
    return jnp.dot(a, b, preferred_element_type=F32)


def product(a, b):
    ah, al = a
    bh, bl = b
    return mul(ah, bh) + (mul(ah, bl) + mul(al, bh))


def shifted(value, axis, by):
    size = lax.axis_size(axis)
    return lax.ppermute(value, axis, [(i, (i + by) % size) for i in range(size)])


def from_behind(value, by):
    size = lax.axis_size(AXES)
    pairs = [(i, i + by) for i in range(size) if 0 <= i + by < size]
    return lax.ppermute(value, AXES, pairs)


def route_kernel(dest_col, dest_row, rows, fluid, out):
    n = dest_row.shape[1]
    earlier = lax.broadcasted_iota(jnp.int32, (n, n), 0) < lax.broadcasted_iota(jnp.int32, (n, n), 1)
    same = (dest_col[...] == dest_row[...]) & earlier
    slot = jnp.sum(jnp.where(same, 1.0, 0.0), axis=0, keepdims=True).astype(jnp.int32)
    target = dest_row[...] * CAP + slot
    q = out.shape[0] * CAP
    selector = jnp.where(lax.broadcasted_iota(jnp.int32, (q, n), 0) == target, 1.0, 0.0).astype(BF16)
    height = fluid.shape[0]
    picked = jnp.where(lax.broadcasted_iota(jnp.int32, (height, n), 0) == rows[...], 1.0, 0.0)
    chosen = lax.dot_general(
        selector, picked.astype(BF16), (((1,), (1,)), ((), ())), preferred_element_type=F32
    ).astype(BF16)
    value = fluid[...]
    high = value.astype(BF16)
    rest = value - high.astype(F32)
    mid = rest.astype(BF16)
    low = (rest - mid.astype(F32)).astype(BF16)
    value = mul(chosen, high) + (mul(chosen, mid) + mul(chosen, low))
    out[...] = value.reshape(out.shape)


def turn_kernel(place, struct, fluid, own_s, send_s, own_f, send_f, held_s, held_f):
    core = place[3]
    held_s[...] = struct[...].T.reshape(held_s.shape)
    held_f[...] = fluid[...].T.reshape(held_f.shape)
    own_s[...] = held_s[:, core]
    send_s[...] = held_s[:, 1 - core]
    own_f[...] = held_f[:, core]
    send_f[...] = held_f[:, 1 - core]


def wet_kernel(coupling, received, out):
    right = received[...].reshape(coupling.shape[1], R)
    out[...] = product(parts(coupling[...]), parts(right))


def gathered(tiles, cols, total, at):
    total[:, at : at + TILE * tiles.shape[0]] = jnp.zeros(
        (total.shape[0], TILE * tiles.shape[0], TILE), F32
    )
    for i in range(tiles.shape[0]):
        rows = pl.ds(at + i * TILE, TILE)
        for k in range(tiles.shape[1]):
            c = cols[i, k]
            total[c, rows] = total[c, rows] + tiles[i, k]


def image(total, pieces):
    acc = None
    c = 0
    for piece in pieces:
        n = piece.shape[0] // TILE
        left = jnp.concatenate([total[c + i] for i in range(n)], axis=1) if n > 1 else total[c]
        term = product(parts(left), parts(piece))
        acc = term if acc is None else acc + term
        c += n
    return acc


def fluid_kernel(cols, stiff, mass, lo, own, hi, after, out, total):
    gathered(stiff, cols, total, 0)
    gathered(mass, cols, total, TILE)
    out[...] = image(total, (lo[...], own[...], hi[...])).reshape(out.shape)


def struct_kernel(cols, stiff, mass, lo, own, hi, after, out, total):
    gathered(stiff, cols, total, 0)
    gathered(mass, cols, total, 2 * TILE)
    out[...] = image(total, (lo[...], own[...], hi[...])).reshape(out.shape)


def joined(one, two):
    return jnp.concatenate([one[...].reshape(R // 2, -1), two[...].reshape(R // 2, -1)], axis=1)


def multiply(held, left, one, two):
    right = jnp.concatenate([one, two], axis=0)
    held[...] = product((left[0][...], left[1][...]), parts(right)).reshape(held.shape)


def send_off(place, held, outs):
    for o in range(4):
        dx = lax.rem(place[0] + o, 4)
        dy = lax.rem(place[1] + o, 4)
        for h in range(2):
            outs[o][0, h] = held[h * 4 + dx, 0:HALF, :]
        outs[4 + o][0] = held[:, HALF:, pl.ds(pl.multiple_of(dy * 256, 256), 256)]


def fluid_product_kernel(place, lf0, lf1, if0, if1, *rest):
    outs, (fh, fl, held) = rest[:8], rest[8:]

    @pl.when(pl.program_id(0) == 0)
    def _():
        fh[...], fl[...] = parts(joined(lf0, lf1))

    multiply(held, (fh, fl), if0[0], if1[0])
    send_off(place, held, outs)


def wet_product_kernel(place, ls0, ls1, ic0, ic1, *rest):
    outs, (sh, sl, held) = rest[8:16], rest[16:]
    sh[...], sl[...] = parts(joined(ls0, ls1))
    multiply(held, (sh, sl), ic0[...], ic1[...])
    send_off(place, held, outs)


def second_kernel(place, ls0, ls1, is0, is1, *rest):
    outs, (sh, sl, held) = rest[:8], rest[8:]

    @pl.when(pl.program_id(0) == 0)
    def _():
        sh[...], sl[...] = parts(joined(ls0, ls1))

    multiply(held, (sh, sl), is0[0], is1[0])
    send_off(place, held, outs)


def split_kernel(axis, place, a0, a1, a2, a3, o0, o1, o2, o3, held):
    held[...] = (a0[...] + a1[...]) + (a2[...] + a3[...])
    for o, out in enumerate((o0, o1, o2, o3)):
        d = lax.rem(place[axis] + o, 4)
        if axis == 1:
            out[...] = held[..., pl.ds(pl.multiple_of(d * 256, 256), 256)]
        else:
            for h in range(2):
                out[:, h] = held[:, h * 4 + d]


def spread_kernel(place, x0, x1, x2, x3, y0, y1, y2, y3, o0, o1, o2, o3, held):
    held[:, :, 0:HALF] = (x0[...] + x1[...]) + (x2[...] + x3[...])
    held[:, :, HALF:] = (y0[...] + y1[...]) + (y2[...] + y3[...])
    for o, out in enumerate((o0, o1, o2, o3)):
        d = lax.rem(place[2] + o, 4)
        lanes = pl.ds(pl.multiple_of(lax.rem(d, 2) * 128, 128), 128)
        out[...] = held[:, d // 2, :, lanes]


def last_kernel(a0, a1, a2, a3, b0, b1, b2, b3, fstiff, fmass, wet, stiff, mass):
    for m, out in enumerate((fstiff, fmass, wet)):
        out[...] = (a0[m] + a1[m]) + (a2[m] + a3[m])
    for m, out in enumerate((stiff, mass)):
        out[...] = (b0[m] + b1[m]) + (b2[m] + b3[m])


def call(kernel, out, count, smem=0, anywhere=0, scratch=(), flops=0, moved=0):
    run = pl.pallas_call(
        kernel,
        out_shape=out,
        in_specs=[SMEM] * smem + [VMEM] * (count - smem - anywhere) + [ANY] * anywhere,
        out_specs=jax.tree.map(lambda _: VMEM, out),
        scratch_shapes=list(scratch),
        compiler_params=PARAMS,
        cost_estimate=pl.CostEstimate(flops=flops, bytes_accessed=moved, transcendentals=0),
    )
    return run


def exchanged(slots, axis):
    return [slots[0]] + [shifted(slots[o], axis, o) for o in range(1, 4)]


def split(place, arrived, axis):
    count = arrived[0].shape[0]
    size = arrived[0].size
    return call(
        functools.partial(split_kernel, axis),
        [shape(count, 2, HALF, 256)] * 4,
        5,
        smem=1,
        scratch=[pltpu.VMEM(arrived[0].shape, F32)],
        flops=3 * size,
        moved=20 * size,
    )(place, *arrived)


def spread(place, x, y):
    count = x[0].shape[0]
    return call(
        spread_kernel,
        [shape(count, 64, 128)] * 4,
        9,
        smem=1,
        scratch=[pltpu.VMEM((count, 2, 64, 256), F32)],
        flops=6 * x[0].size,
        moved=40 * x[0].size,
    )(place, *x, *y)


def partial_sums(kernel, steps, at, count, place, lefts, depth, operands, specs, carried=()):
    left = pltpu.VMEM((512, depth), BF16)
    run = pl.pallas_call(
        kernel,
        grid=(steps,),
        out_shape=[shape(count, 2, HALF, R)] * 4 + [shape(count, 8, HALF, 256)] * 4,
        in_specs=[SMEM] + [VMEM] * len(lefts) + specs + [ANY] * len(carried),
        out_specs=[pl.BlockSpec((1, 2, HALF, R), lambda m: (m + at, 0, 0, 0))] * 4
        + [pl.BlockSpec((1, 8, HALF, 256), lambda m: (m + at, 0, 0, 0))] * 4,
        scratch_shapes=[left, left, pltpu.VMEM((8, 64, R), F32)],
        input_output_aliases={1 + len(lefts) + len(specs) + i: i for i in range(len(carried))},
        compiler_params=PARAMS,
        cost_estimate=pl.CostEstimate(
            flops=6 * steps * 512 * depth * R, bytes_accessed=4 * steps * 2**20, transcendentals=0
        ),
    )
    return run(place, *lefts, *operands, *carried)


def compute(
    struct_basis,
    fluid_basis,
    stiff_tiles,
    mass_tiles,
    fluid_stiff_tiles,
    fluid_mass_tiles,
    struct_cols,
    fluid_cols,
    wet_rows,
    wet_dest,
    coupling,
):
    place = jnp.stack([lax.axis_index(X), lax.axis_index(Y), lax.axis_index(Z), lax.axis_index("core")]).astype(
        jnp.int32
    )
    below_s = from_behind(struct_basis[-TILE:], 1)
    above_s = from_behind(struct_basis[:TILE], -1)
    below_f = from_behind(fluid_basis, 1)
    above_f = from_behind(fluid_basis, -1)

    outgoing = call(route_kernel, shape(128, CAP, R), 4, flops=2 * 3 * 256 * 128 * R, moved=2**21)(
        wet_dest, wet_dest.reshape(1, -1), wet_rows.reshape(1, -1), fluid_basis
    )
    received = lax.all_to_all(outgoing, AXES, split_axis=0, concat_axis=0, tiled=True)

    own_s, send_s, own_f, send_f = call(
        turn_kernel,
        [shape(8, 64, 256)] * 2 + [shape(8, 64, 128)] * 2,
        3,
        smem=1,
        scratch=[pltpu.VMEM((8, 2, 64, 256), F32), pltpu.VMEM((8, 2, 64, 128), F32)],
        flops=2**20,
        moved=3 * 2**20,
    )(place, struct_basis, fluid_basis)
    left_s = shifted(send_s, "core", 1)
    left_f = shifted(send_f, "core", 1)

    image_c = call(wet_kernel, shape(256, R), 2, flops=6 * 256 * 256 * R, moved=2**21)(coupling, received)
    other_c = shifted(image_c, "core", 1)

    image_f = call(
        fluid_kernel,
        shape(2, 128, R),
        7,
        smem=1,
        anywhere=1,
        scratch=[pltpu.VMEM((3, 256, TILE), F32)],
        flops=6 * 256 * 384 * R,
        moved=3 * 2**20,
    )(fluid_cols, fluid_stiff_tiles, fluid_mass_tiles, below_f, fluid_basis, above_f, own_s)
    other_f = shifted(image_f, "core", 1)

    def block(rows):
        return pl.BlockSpec((1, rows, R), lambda m: (m, 0, 0))

    fluid = partial_sums(
        fluid_product_kernel, 2, 0, 3, place, (own_f, left_f), 256, (image_f, other_f), [block(128)] * 2
    )
    first = partial_sums(
        wet_product_kernel, 1, 2, 3, place, (own_s, left_s), 512, (image_c, other_c), [VMEM] * 2, fluid
    )
    first_x = exchanged(first[0:4], X)
    first_y = exchanged(first[4:8], Y)

    image_s = call(
        struct_kernel,
        shape(2, 256, R),
        7,
        smem=1,
        anywhere=1,
        scratch=[pltpu.VMEM((4, 512, TILE), F32)],
        flops=6 * 512 * 512 * R,
        moved=5 * 2**20,
    )(struct_cols, stiff_tiles, mass_tiles, below_s, struct_basis, above_s, first[0])
    other_s = shifted(image_s, "core", 1)

    second = partial_sums(second_kernel, 2, 0, 2, place, (own_s, left_s), 512, (image_s, other_s), [block(256)] * 2)
    second_x = exchanged(second[0:4], X)
    second_y = exchanged(second[4:8], Y)

    first_xy = exchanged(split(place, first_x, 1), Y)
    first_yx = exchanged(split(place, first_y, 0), X)
    second_xy = exchanged(split(place, second_x, 1), Y)
    second_yx = exchanged(split(place, second_y, 0), X)
    first_z = exchanged(spread(place, first_xy, first_yx), Z)
    second_z = exchanged(spread(place, second_xy, second_yx), Z)
    fstiff, fmass, wet, stiff, mass = call(
        last_kernel, [shape(64, 128)] * 5, 8, flops=2**18, moved=2**20
    )(*first_z, *second_z)
    return stiff, mass, fstiff, fmass, wet


def solution(mesh):
    fine = Mesh(mesh.devices.reshape(2, 4, 2, 4, 2), AXES)
    return jax.shard_map(
        compute,
        mesh=fine,
        in_specs=(
            P(AXES, None),
            P(AXES, None),
            P(AXES, None, None, None),
            P(AXES, None, None, None),
            P(AXES, None, None, None),
            P(AXES, None, None, None),
            P(AXES, None),
            P(AXES, None),
            P(AXES),
            P(AXES, None),
            P(AXES, None),
        ),
        out_specs=(P(ROW, COL),) * 5,
        check_vma=False,
    )
```

```python
import functools

import jax
import jax.numpy as jnp
from jax import lax
from jax.experimental import pallas as pl
from jax.experimental.pallas import tpu as pltpu
from jax.sharding import Mesh
from jax.sharding import PartitionSpec as P


R = 1024
TILE = 128
CAP = 2
F32 = jnp.float32
BF16 = jnp.bfloat16

AXES = ("zhi", "x", "core", "y", "zlo")
ROW = ("zhi", "x", "core")
COL = ("y", "zlo")
X, Y, Z = "x", "y", ("zhi", "zlo")
HALF = 32


VMEM = pl.BlockSpec(memory_space=pltpu.VMEM)
SMEM = pl.BlockSpec(memory_space=pltpu.SMEM)
ANY = pl.BlockSpec(memory_space=pl.ANY)
PARAMS = pltpu.CompilerParams(vmem_limit_bytes=60 * 1024 * 1024)


def shape(*dims):
    return jax.ShapeDtypeStruct(dims, F32)


def parts(value):
    high = value.astype(BF16)
    low = (value - high.astype(F32)).astype(BF16)
    return high, low


def mul(a, b):
    return jnp.dot(a, b, preferred_element_type=F32)


def product(a, b):
    ah, al = a
    bh, bl = b
    return mul(ah, bh) + (mul(ah, bl) + mul(al, bh))


def shifted(value, axis, by):
    size = lax.axis_size(axis)
    return lax.ppermute(value, axis, [(i, (i + by) % size) for i in range(size)])


def from_behind(value, by):
    size = lax.axis_size(AXES)
    pairs = [(i, i + by) for i in range(size) if 0 <= i + by < size]
    return lax.ppermute(value, AXES, pairs)


def route_kernel(dest_row, rows, fluid, out):
    n = dest_row.shape[1]
    dest = jnp.broadcast_to(dest_row[...].astype(F32), (n, n))
    earlier = lax.broadcasted_iota(jnp.int32, (n, n), 0) < lax.broadcasted_iota(jnp.int32, (n, n), 1)
    same = (dest.T == dest) & earlier
    slot = jnp.sum(jnp.where(same, 1.0, 0.0), axis=0, keepdims=True).astype(jnp.int32)
    target = dest_row[...] * CAP + slot
    q = out.shape[0] * CAP
    selector = jnp.where(lax.broadcasted_iota(jnp.int32, (q, n), 0) == target, 1.0, 0.0).astype(BF16)
    height = fluid.shape[0]
    picked = jnp.where(lax.broadcasted_iota(jnp.int32, (height, n), 0) == rows[...], 1.0, 0.0)
    chosen = lax.dot_general(
        selector, picked.astype(BF16), (((1,), (1,)), ((), ())), preferred_element_type=F32
    ).astype(BF16)
    value = fluid[...]
    high = value.astype(BF16)
    rest = value - high.astype(F32)
    mid = rest.astype(BF16)
    low = (rest - mid.astype(F32)).astype(BF16)
    value = mul(chosen, high) + (mul(chosen, mid) + mul(chosen, low))
    out[...] = value.reshape(out.shape)


def turn_kernel(place, struct, fluid, own_s, send_s, own_f, send_f, held_s, held_f):
    core = place[3]
    held_s[...] = struct[...].T.reshape(held_s.shape)
    held_f[...] = fluid[...].T.reshape(held_f.shape)
    own_s[...] = held_s[:, core]
    send_s[...] = held_s[:, 1 - core]
    own_f[...] = held_f[:, core]
    send_f[...] = held_f[:, 1 - core]


def wet_kernel(coupling, received, out):
    right = received[...].reshape(coupling.shape[1], R)
    out[...] = product(parts(coupling[...]), parts(right))


def gathered(tiles, cols, total, at):
    total[:, at : at + TILE * tiles.shape[0]] = jnp.zeros(
        (total.shape[0], TILE * tiles.shape[0], TILE), F32
    )
    for i in range(tiles.shape[0]):
        rows = pl.ds(at + i * TILE, TILE)
        for k in range(tiles.shape[1]):
            c = cols[i, k]
            total[c, rows] = total[c, rows] + tiles[i, k]


def image(total, pieces):
    acc = None
    c = 0
    for piece in pieces:
        n = piece.shape[0] // TILE
        left = jnp.concatenate([total[c + i] for i in range(n)], axis=1) if n > 1 else total[c]
        term = product(parts(left), parts(piece))
        acc = term if acc is None else acc + term
        c += n
    return acc


def fluid_kernel(cols, stiff, mass, lo, own, hi, after, out, total):
    gathered(stiff, cols, total, 0)
    gathered(mass, cols, total, TILE)
    out[...] = image(total, (lo[...], own[...], hi[...])).reshape(out.shape)


def struct_kernel(cols, stiff, mass, lo, own, hi, after, out, total):
    gathered(stiff, cols, total, 0)
    gathered(mass, cols, total, 2 * TILE)
    out[...] = image(total, (lo[...], own[...], hi[...])).reshape(out.shape)


def joined(one, two):
    return jnp.concatenate([one[...].reshape(R // 2, -1), two[...].reshape(R // 2, -1)], axis=1)


def multiply(held, left, one, two):
    right = jnp.concatenate([one, two], axis=0)
    held[...] = product((left[0][...], left[1][...]), parts(right)).reshape(held.shape)


def send_off(place, held, outs):
    for o in range(4):
        dx = lax.rem(place[0] + o, 4)
        dy = lax.rem(place[1] + o, 4)
        for h in range(2):
            outs[o][0, h] = held[h * 4 + dx, 0:HALF, :]
        outs[4 + o][0] = held[:, HALF:, pl.ds(pl.multiple_of(dy * 256, 256), 256)]


def fluid_product_kernel(place, lf0, lf1, if0, if1, *rest):
    outs, (fh, fl, held) = rest[:8], rest[8:]

    @pl.when(pl.program_id(0) == 0)
    def _():
        fh[...], fl[...] = parts(joined(lf0, lf1))

    multiply(held, (fh, fl), if0[0], if1[0])
    send_off(place, held, outs)


def wet_product_kernel(place, ls0, ls1, ic0, ic1, *rest):
    outs, (sh, sl, held) = rest[:8], rest[8:]
    sh[...], sl[...] = parts(joined(ls0, ls1))
    multiply(held, (sh, sl), ic0[...], ic1[...])
    send_off(place, held, outs)


def second_kernel(place, ls0, ls1, is0, is1, *rest):
    outs, (sh, sl, held) = rest[8:16], rest[16:]

    @pl.when(pl.program_id(0) == 0)
    def _():
        sh[...], sl[...] = parts(joined(ls0, ls1))

    multiply(held, (sh, sl), is0[0], is1[0])
    send_off(place, held, outs)


def split_kernel(axis, place, a0, a1, a2, a3, o0, o1, o2, o3, held):
    held[...] = (a0[...] + a1[...]) + (a2[...] + a3[...])
    for o, out in enumerate((o0, o1, o2, o3)):
        d = lax.rem(place[axis] + o, 4)
        if axis == 1:
            out[...] = held[..., pl.ds(pl.multiple_of(d * 256, 256), 256)]
        else:
            for h in range(2):
                out[:, h] = held[:, h * 4 + d]


def spread_kernel(place, *refs):
    ins, outs, held = refs[:16], refs[16:20], refs[20]
    at = 0
    for x, y in ((ins[0:4], ins[4:8]), (ins[8:12], ins[12:16])):
        rows = slice(at, at + x[0].shape[0])
        held[rows, :, 0:HALF] = (x[0][...] + x[1][...]) + (x[2][...] + x[3][...])
        held[rows, :, HALF:] = (y[0][...] + y[1][...]) + (y[2][...] + y[3][...])
        at = rows.stop
    for o, out in enumerate(outs):
        d = lax.rem(place[2] + o, 4)
        lanes = pl.ds(pl.multiple_of(lax.rem(d, 2) * 128, 128), 128)
        out[...] = held[:, d // 2, :, lanes]


def last_kernel(a0, a1, a2, a3, *outs):
    for m, out in enumerate(outs):
        out[...] = (a0[m] + a1[m]) + (a2[m] + a3[m])


def call(kernel, out, count, smem=0, anywhere=0, scratch=(), flops=0, moved=0):
    run = pl.pallas_call(
        kernel,
        out_shape=out,
        in_specs=[SMEM] * smem + [VMEM] * (count - smem - anywhere) + [ANY] * anywhere,
        out_specs=jax.tree.map(lambda _: VMEM, out),
        scratch_shapes=list(scratch),
        compiler_params=PARAMS,
        cost_estimate=pl.CostEstimate(flops=flops, bytes_accessed=moved, transcendentals=0),
    )
    return run


def exchanged(slots, axis):
    return [slots[0]] + [shifted(slots[o], axis, o) for o in range(1, 4)]


def split(place, arrived, axis):
    count = arrived[0].shape[0]
    size = arrived[0].size
    return call(
        functools.partial(split_kernel, axis),
        [shape(count, 2, HALF, 256)] * 4,
        5,
        smem=1,
        scratch=[pltpu.VMEM(arrived[0].shape, F32)],
        flops=3 * size,
        moved=20 * size,
    )(place, *arrived)


def spread(place, *arrived):
    return call(
        spread_kernel,
        [shape(5, 64, 128)] * 4,
        17,
        smem=1,
        scratch=[pltpu.VMEM((5, 2, 64, 256), F32)],
        flops=2**20,
        moved=2**22,
    )(place, *arrived)


def partial_sums(kernel, steps, at, count, place, lefts, depth, operands, specs, carried=()):
    left = pltpu.VMEM((512, depth), BF16)
    run = pl.pallas_call(
        kernel,
        grid=(steps,),
        out_shape=[shape(count, 2, HALF, R)] * 4 + [shape(count, 8, HALF, 256)] * 4,
        in_specs=[SMEM] + [VMEM] * len(lefts) + specs + [ANY] * len(carried),
        out_specs=[pl.BlockSpec((1, 2, HALF, R), lambda m: (m + at, 0, 0, 0))] * 4
        + [pl.BlockSpec((1, 8, HALF, 256), lambda m: (m + at, 0, 0, 0))] * 4,
        scratch_shapes=[left, left, pltpu.VMEM((8, 64, R), F32)],
        input_output_aliases={1 + len(lefts) + len(specs) + i: i for i in range(len(carried))},
        compiler_params=PARAMS,
        cost_estimate=pl.CostEstimate(
            flops=6 * steps * 512 * depth * R, bytes_accessed=4 * steps * 2**20, transcendentals=0
        ),
    )
    return run(place, *lefts, *operands, *carried)


def compute(
    struct_basis,
    fluid_basis,
    stiff_tiles,
    mass_tiles,
    fluid_stiff_tiles,
    fluid_mass_tiles,
    struct_cols,
    fluid_cols,
    wet_rows,
    wet_dest,
    coupling,
):
    place = jnp.stack([lax.axis_index(X), lax.axis_index(Y), lax.axis_index(Z), lax.axis_index("core")]).astype(
        jnp.int32
    )
    below_s = from_behind(struct_basis[-TILE:], 1)
    above_s = from_behind(struct_basis[:TILE], -1)
    below_f = from_behind(fluid_basis, 1)
    above_f = from_behind(fluid_basis, -1)

    outgoing = call(route_kernel, shape(128, CAP, R), 3, flops=2 * 3 * 256 * 128 * R, moved=2**21)(
        wet_dest.reshape(1, -1), wet_rows.reshape(1, -1), fluid_basis
    )
    received = lax.all_to_all(outgoing, AXES, split_axis=0, concat_axis=0, tiled=True)

    own_s, send_s, own_f, send_f = call(
        turn_kernel,
        [shape(8, 64, 256)] * 2 + [shape(8, 64, 128)] * 2,
        3,
        smem=1,
        scratch=[pltpu.VMEM((8, 2, 64, 256), F32), pltpu.VMEM((8, 2, 64, 128), F32)],
        flops=2**20,
        moved=3 * 2**20,
    )(place, struct_basis, fluid_basis)
    left_s = shifted(send_s, "core", 1)
    left_f = shifted(send_f, "core", 1)

    image_c = call(wet_kernel, shape(256, R), 2, flops=6 * 256 * 256 * R, moved=2**21)(coupling, received)
    other_c = shifted(image_c, "core", 1)

    image_f = call(
        fluid_kernel,
        shape(2, 128, R),
        7,
        smem=1,
        anywhere=1,
        scratch=[pltpu.VMEM((3, 256, TILE), F32)],
        flops=6 * 256 * 384 * R,
        moved=3 * 2**20,
    )(fluid_cols, fluid_stiff_tiles, fluid_mass_tiles, below_f, fluid_basis, above_f, own_s)
    other_f = shifted(image_f, "core", 1)

    def block(rows):
        return pl.BlockSpec((1, rows, R), lambda m: (m, 0, 0))

    first = partial_sums(
        fluid_product_kernel, 2, 0, 2, place, (own_f, left_f), 256, (image_f, other_f), [block(128)] * 2
    )
    first_x = exchanged(first[0:4], X)
    first_y = exchanged(first[4:8], Y)

    image_s = call(
        struct_kernel,
        shape(2, 256, R),
        7,
        smem=1,
        anywhere=1,
        scratch=[pltpu.VMEM((4, 512, TILE), F32)],
        flops=6 * 512 * 512 * R,
        moved=5 * 2**20,
    )(struct_cols, stiff_tiles, mass_tiles, below_s, struct_basis, above_s, first[0])
    other_s = shifted(image_s, "core", 1)

    wet = partial_sums(wet_product_kernel, 1, 2, 3, place, (own_s, left_s), 512, (image_c, other_c), [VMEM] * 2)
    second = partial_sums(
        second_kernel, 2, 0, 3, place, (own_s, left_s), 512, (image_s, other_s), [block(256)] * 2, wet
    )
    second_x = exchanged(second[0:4], X)
    second_y = exchanged(second[4:8], Y)

    first_xy = exchanged(split(place, first_x, 1), Y)
    first_yx = exchanged(split(place, first_y, 0), X)
    second_xy = exchanged(split(place, second_x, 1), Y)
    second_yx = exchanged(split(place, second_y, 0), X)
    summed = exchanged(spread(place, *first_xy, *first_yx, *second_xy, *second_yx), Z)
    fstiff, fmass, stiff, mass, wet = call(last_kernel, [shape(64, 128)] * 5, 4, flops=2**18, moved=2**20)(*summed)
    return stiff, mass, fstiff, fmass, wet


def solution(mesh):
    fine = Mesh(mesh.devices.reshape(2, 4, 2, 4, 2), AXES)
    return jax.shard_map(
        compute,
        mesh=fine,
        in_specs=(
            P(AXES, None),
            P(AXES, None),
            P(AXES, None, None, None),
            P(AXES, None, None, None),
            P(AXES, None, None, None),
            P(AXES, None, None, None),
            P(AXES, None),
            P(AXES, None),
            P(AXES),
            P(AXES, None),
            P(AXES, None),
        ),
        out_specs=(P(ROW, COL),) * 5,
        check_vma=False,
    )
```

```python
import jax
import jax.numpy as jnp
from jax import lax
from jax.experimental import pallas as pl
from jax.experimental.pallas import tpu as pltpu
from jax.sharding import Mesh
from jax.sharding import PartitionSpec as P


R = 1024
TILE = 128
CAP = 2
F32 = jnp.float32
BF16 = jnp.bfloat16

AXES = ("zhi", "x", "core", "y", "zlo")
ROW = ("zhi", "x", "core")
COL = ("y", "zlo")
X, Y, Z = "x", "y", ("zhi", "zlo")
HALF = 32


VMEM = pl.BlockSpec(memory_space=pltpu.VMEM)
SMEM = pl.BlockSpec(memory_space=pltpu.SMEM)
ANY = pl.BlockSpec(memory_space=pl.ANY)
PARAMS = pltpu.CompilerParams(vmem_limit_bytes=60 * 1024 * 1024)


def shape(*dims):
    return jax.ShapeDtypeStruct(dims, F32)


def parts(value):
    high = value.astype(BF16)
    low = (value - high.astype(F32)).astype(BF16)
    return high, low


def mul(a, b):
    return jnp.dot(a, b, preferred_element_type=F32)


def product(a, b):
    ah, al = a
    bh, bl = b
    return mul(ah, bh) + (mul(ah, bl) + mul(al, bh))


def shifted(value, axis, by):
    size = lax.axis_size(axis)
    return lax.ppermute(value, axis, [(i, (i + by) % size) for i in range(size)])


def from_behind(value, by):
    size = lax.axis_size(AXES)
    pairs = [(i, i + by) for i in range(size) if 0 <= i + by < size]
    return lax.ppermute(value, AXES, pairs)


def route_kernel(dest_row, rows, fluid, out):
    n = dest_row.shape[1]
    dest = jnp.broadcast_to(dest_row[...].astype(F32), (n, n))
    earlier = lax.broadcasted_iota(jnp.int32, (n, n), 0) < lax.broadcasted_iota(jnp.int32, (n, n), 1)
    same = (dest.T == dest) & earlier
    slot = jnp.sum(jnp.where(same, 1.0, 0.0), axis=0, keepdims=True).astype(jnp.int32)
    target = dest_row[...] * CAP + slot
    q = out.shape[0] * CAP
    selector = jnp.where(lax.broadcasted_iota(jnp.int32, (q, n), 0) == target, 1.0, 0.0).astype(BF16)
    height = fluid.shape[0]
    picked = jnp.where(lax.broadcasted_iota(jnp.int32, (height, n), 0) == rows[...], 1.0, 0.0)
    chosen = lax.dot_general(
        selector, picked.astype(BF16), (((1,), (1,)), ((), ())), preferred_element_type=F32
    ).astype(BF16)
    value = fluid[...]
    high = value.astype(BF16)
    rest = value - high.astype(F32)
    mid = rest.astype(BF16)
    low = (rest - mid.astype(F32)).astype(BF16)
    value = mul(chosen, high) + (mul(chosen, mid) + mul(chosen, low))
    out[...] = value.reshape(out.shape)


def turn_kernel(place, struct, fluid, own_s, send_s, own_f, send_f, held_s, held_f):
    core = place[3]
    held_s[...] = struct[...].T.reshape(held_s.shape)
    held_f[...] = fluid[...].T.reshape(held_f.shape)
    own_s[...] = held_s[:, core]
    send_s[...] = held_s[:, 1 - core]
    own_f[...] = held_f[:, core]
    send_f[...] = held_f[:, 1 - core]


def wet_kernel(coupling, received, out):
    right = received[...].reshape(coupling.shape[1], R)
    out[...] = product(parts(coupling[...]), parts(right))


def gathered(tiles, cols, total, at):
    total[:, at : at + TILE * tiles.shape[0]] = jnp.zeros(
        (total.shape[0], TILE * tiles.shape[0], TILE), F32
    )
    for i in range(tiles.shape[0]):
        rows = pl.ds(at + i * TILE, TILE)
        for k in range(tiles.shape[1]):
            c = cols[i, k]
            total[c, rows] = total[c, rows] + tiles[i, k]


def image(total, pieces):
    acc = None
    c = 0
    for piece in pieces:
        n = piece.shape[0] // TILE
        left = jnp.concatenate([total[c + i] for i in range(n)], axis=1) if n > 1 else total[c]
        term = product(parts(left), parts(piece))
        acc = term if acc is None else acc + term
        c += n
    return acc


def fluid_kernel(cols, stiff, mass, lo, own, hi, after, out, total):
    gathered(stiff, cols, total, 0)
    gathered(mass, cols, total, TILE)
    out[...] = image(total, (lo[...], own[...], hi[...])).reshape(out.shape)


def struct_kernel(cols, stiff, mass, lo, own, hi, after, out, total):
    gathered(stiff, cols, total, 0)
    gathered(mass, cols, total, 2 * TILE)
    out[...] = image(total, (lo[...], own[...], hi[...])).reshape(out.shape)


def joined(one, two):
    return jnp.concatenate([one[...].reshape(R // 2, -1), two[...].reshape(R // 2, -1)], axis=1)


def multiply(held, left, one, two):
    right = jnp.concatenate([one, two], axis=0)
    held[...] = product((left[0][...], left[1][...]), parts(right)).reshape(held.shape)


def along_x(place, held, rows, outs):
    for o, out in enumerate(outs):
        d = lax.rem(place[0] + o, 4)
        for h in range(2):
            out[0, h] = held[h * 4 + d, rows, :]


def along_y(place, held, rows, outs):
    for o, out in enumerate(outs):
        d = lax.rem(place[1] + o, 4)
        out[0] = held[:, rows, pl.ds(pl.multiple_of(d * 256, 256), 256)]


def fluid_product_kernel(place, lf0, lf1, if0, if1, o0, o1, o2, o3, fh, fl, held):
    @pl.when(pl.program_id(0) == 0)
    def _():
        fh[...], fl[...] = parts(joined(lf0, lf1))

    multiply(held, (fh, fl), if0[0], if1[0])
    along_x(place, held, slice(0, 64), (o0, o1, o2, o3))


def wet_product_kernel(place, ls0, ls1, ic0, ic1, o0, o1, o2, o3, sh, sl, held):
    sh[...], sl[...] = parts(joined(ls0, ls1))
    multiply(held, (sh, sl), ic0[...], ic1[...])
    along_y(place, held, slice(0, 64), (o0, o1, o2, o3))


def second_kernel(place, ls0, ls1, is0, is1, *rest):
    outs, (sh, sl, held) = rest[:8], rest[8:]

    @pl.when(pl.program_id(0) == 0)
    def _():
        sh[...], sl[...] = parts(joined(ls0, ls1))

    multiply(held, (sh, sl), is0[0], is1[0])
    along_x(place, held, slice(0, HALF), outs[:4])
    along_y(place, held, slice(HALF, 64), outs[4:])


def to_y_kernel(place, a0, a1, a2, a3, o0, o1, o2, o3, held):
    held[...] = (a0[...] + a1[...]) + (a2[...] + a3[...])
    for o, out in enumerate((o0, o1, o2, o3)):
        d = lax.rem(place[1] + o, 4)
        out[...] = held[..., pl.ds(pl.multiple_of(d * 256, 256), 256)]


def to_x_kernel(place, a0, a1, a2, a3, b0, b1, b2, b3, o0, o1, o2, o3, held):
    held[0:2] = (a0[...] + a1[...]) + (a2[...] + a3[...])
    for k in range(2):
        rows = slice(k * HALF, (k + 1) * HALF)
        held[2 + k] = (b0[0, :, rows] + b1[0, :, rows]) + (b2[0, :, rows] + b3[0, :, rows])
    for o, out in enumerate((o0, o1, o2, o3)):
        d = lax.rem(place[0] + o, 4)
        for h in range(2):
            out[:, h] = held[:, h * 4 + d]


def spread_kernel(place, *refs):
    f, x, y, outs, held = refs[0:4], refs[4:8], refs[8:12], refs[12:16], refs[16]
    held[0:2] = (f[0][...] + f[1][...]) + (f[2][...] + f[3][...])
    held[2:4, :, 0:HALF] = (x[0][...] + x[1][...]) + (x[2][...] + x[3][...])
    for m, k, at in ((2, 0, HALF), (3, 1, HALF), (4, 2, 0), (4, 3, HALF)):
        held[m, :, at : at + HALF] = (y[0][k] + y[1][k]) + (y[2][k] + y[3][k])
    for o, out in enumerate(outs):
        d = lax.rem(place[2] + o, 4)
        lanes = pl.ds(pl.multiple_of(lax.rem(d, 2) * 128, 128), 128)
        out[...] = held[:, d // 2, :, lanes]


def last_kernel(a0, a1, a2, a3, *outs):
    for m, out in enumerate(outs):
        out[...] = (a0[m] + a1[m]) + (a2[m] + a3[m])


def call(kernel, out, count, smem=0, anywhere=0, scratch=(), flops=0, moved=0):
    run = pl.pallas_call(
        kernel,
        out_shape=out,
        in_specs=[SMEM] * smem + [VMEM] * (count - smem - anywhere) + [ANY] * anywhere,
        out_specs=jax.tree.map(lambda _: VMEM, out),
        scratch_shapes=list(scratch),
        compiler_params=PARAMS,
        cost_estimate=pl.CostEstimate(flops=flops, bytes_accessed=moved, transcendentals=0),
    )
    return run


def exchanged(slots, axis):
    return [slots[0]] + [shifted(slots[o], axis, o) for o in range(1, 4)]


def split(kernel, place, arrived, out, held):
    size = sum(a.size for a in arrived)
    return call(
        kernel, [shape(*out)] * 4, 1 + len(arrived), smem=1, scratch=[pltpu.VMEM(held, F32)], flops=size, moved=5 * size
    )(place, *arrived)


def spread(place, *arrived):
    return call(
        spread_kernel,
        [shape(5, 64, 128)] * 4,
        13,
        smem=1,
        scratch=[pltpu.VMEM((5, 2, 64, 256), F32)],
        flops=2**20,
        moved=2**22,
    )(place, *arrived)


def partial_sums(kernel, steps, place, lefts, depth, operands, specs, x_rows, y_rows):
    left = pltpu.VMEM((512, depth), BF16)
    outs = [(2, x_rows, R)] * 4 * (x_rows > 0) + [(8, y_rows, 256)] * 4 * (y_rows > 0)
    run = pl.pallas_call(
        kernel,
        grid=(steps,),
        out_shape=[shape(steps, *dims) for dims in outs],
        in_specs=[SMEM] + [VMEM] * len(lefts) + specs,
        out_specs=[pl.BlockSpec((1, *dims), lambda m: (m, 0, 0, 0)) for dims in outs],
        scratch_shapes=[left, left, pltpu.VMEM((8, 64, R), F32)],
        compiler_params=PARAMS,
        cost_estimate=pl.CostEstimate(
            flops=6 * steps * 512 * depth * R, bytes_accessed=4 * steps * 2**20, transcendentals=0
        ),
    )
    return run(place, *lefts, *operands)


def compute(
    struct_basis,
    fluid_basis,
    stiff_tiles,
    mass_tiles,
    fluid_stiff_tiles,
    fluid_mass_tiles,
    struct_cols,
    fluid_cols,
    wet_rows,
    wet_dest,
    coupling,
):
    place = jnp.stack([lax.axis_index(X), lax.axis_index(Y), lax.axis_index(Z), lax.axis_index("core")]).astype(
        jnp.int32
    )
    below_s = from_behind(struct_basis[-TILE:], 1)
    above_s = from_behind(struct_basis[:TILE], -1)
    below_f = from_behind(fluid_basis, 1)
    above_f = from_behind(fluid_basis, -1)

    outgoing = call(route_kernel, shape(128, CAP, R), 3, flops=2 * 3 * 256 * 128 * R, moved=2**21)(
        wet_dest.reshape(1, -1), wet_rows.reshape(1, -1), fluid_basis
    )
    received = lax.all_to_all(outgoing, AXES, split_axis=0, concat_axis=0, tiled=True)

    own_s, send_s, own_f, send_f = call(
        turn_kernel,
        [shape(8, 64, 256)] * 2 + [shape(8, 64, 128)] * 2,
        3,
        smem=1,
        scratch=[pltpu.VMEM((8, 2, 64, 256), F32), pltpu.VMEM((8, 2, 64, 128), F32)],
        flops=2**20,
        moved=3 * 2**20,
    )(place, struct_basis, fluid_basis)
    left_s = shifted(send_s, "core", 1)
    left_f = shifted(send_f, "core", 1)

    image_c = call(wet_kernel, shape(256, R), 2, flops=6 * 256 * 256 * R, moved=2**21)(coupling, received)
    other_c = shifted(image_c, "core", 1)

    image_f = call(
        fluid_kernel,
        shape(2, 128, R),
        7,
        smem=1,
        anywhere=1,
        scratch=[pltpu.VMEM((3, 256, TILE), F32)],
        flops=6 * 256 * 384 * R,
        moved=3 * 2**20,
    )(fluid_cols, fluid_stiff_tiles, fluid_mass_tiles, below_f, fluid_basis, above_f, own_s)
    other_f = shifted(image_f, "core", 1)

    def block(rows):
        return pl.BlockSpec((1, rows, R), lambda m: (m, 0, 0))

    fluid = partial_sums(
        fluid_product_kernel, 2, place, (own_f, left_f), 256, (image_f, other_f), [block(128)] * 2, 64, 0
    )
    fluid_x = exchanged(fluid, X)

    image_s = call(
        struct_kernel,
        shape(2, 256, R),
        7,
        smem=1,
        anywhere=1,
        scratch=[pltpu.VMEM((4, 512, TILE), F32)],
        flops=6 * 512 * 512 * R,
        moved=5 * 2**20,
    )(struct_cols, stiff_tiles, mass_tiles, below_s, struct_basis, above_s, fluid[0])
    other_s = shifted(image_s, "core", 1)

    coupled = partial_sums(wet_product_kernel, 1, place, (own_s, left_s), 512, (image_c, other_c), [VMEM] * 2, 0, 64)
    coupled_y = exchanged(coupled, Y)
    struct = partial_sums(
        second_kernel, 2, place, (own_s, left_s), 512, (image_s, other_s), [block(256)] * 2, HALF, HALF
    )
    struct_x = exchanged(struct[0:4], X)
    struct_y = exchanged(struct[4:8], Y)

    fluid_xy = exchanged(split(to_y_kernel, place, fluid_x, (2, 2, 64, 256), (2, 2, 64, R)), Y)
    struct_xy = exchanged(split(to_y_kernel, place, struct_x, (2, 2, HALF, 256), (2, 2, HALF, R)), Y)
    both_yx = exchanged(split(to_x_kernel, place, struct_y + coupled_y, (4, 2, HALF, 256), (4, 8, HALF, 256)), X)
    summed = exchanged(spread(place, *fluid_xy, *struct_xy, *both_yx), Z)
    fstiff, fmass, stiff, mass, wet = call(last_kernel, [shape(64, 128)] * 5, 4, flops=2**18, moved=2**20)(*summed)
    return stiff, mass, fstiff, fmass, wet


def solution(mesh):
    fine = Mesh(mesh.devices.reshape(2, 4, 2, 4, 2), AXES)
    return jax.shard_map(
        compute,
        mesh=fine,
        in_specs=(
            P(AXES, None),
            P(AXES, None),
            P(AXES, None, None, None),
            P(AXES, None, None, None),
            P(AXES, None, None, None),
            P(AXES, None, None, None),
            P(AXES, None),
            P(AXES, None),
            P(AXES),
            P(AXES, None),
            P(AXES, None),
        ),
        out_specs=(P(ROW, COL),) * 5,
        check_vma=False,
    )
```

```python
import jax
import jax.numpy as jnp
from jax import lax
from jax.experimental import pallas as pl
from jax.experimental.pallas import tpu as pltpu
from jax.sharding import Mesh
from jax.sharding import PartitionSpec as P


R = 1024
TILE = 128
CAP = 2
F32 = jnp.float32
BF16 = jnp.bfloat16

AXES = ("zhi", "x", "core", "y", "zlo")
ROW = ("zhi", "x", "core")
COL = ("y", "zlo")
X, Y, Z = "x", "y", ("zhi", "zlo")
NX = 24
NY = 40


VMEM = pl.BlockSpec(memory_space=pltpu.VMEM)
SMEM = pl.BlockSpec(memory_space=pltpu.SMEM)
ANY = pl.BlockSpec(memory_space=pl.ANY)
PARAMS = pltpu.CompilerParams(vmem_limit_bytes=60 * 1024 * 1024)


def shape(*dims):
    return jax.ShapeDtypeStruct(dims, F32)


def parts(value):
    high = value.astype(BF16)
    low = (value - high.astype(F32)).astype(BF16)
    return high, low


def mul(a, b):
    return jnp.dot(a, b, preferred_element_type=F32)


def product(a, b):
    ah, al = a
    bh, bl = b
    return mul(ah, bh) + (mul(ah, bl) + mul(al, bh))


def shifted(value, axis, by):
    size = lax.axis_size(axis)
    return lax.ppermute(value, axis, [(i, (i + by) % size) for i in range(size)])


def from_behind(value, by):
    size = lax.axis_size(AXES)
    pairs = [(i, i + by) for i in range(size) if 0 <= i + by < size]
    return lax.ppermute(value, AXES, pairs)


def route_kernel(dest_row, rows, fluid, out):
    n = dest_row.shape[1]
    dest = jnp.broadcast_to(dest_row[...].astype(F32), (n, n))
    earlier = lax.broadcasted_iota(jnp.int32, (n, n), 0) < lax.broadcasted_iota(jnp.int32, (n, n), 1)
    same = (dest.T == dest) & earlier
    slot = jnp.sum(jnp.where(same, 1.0, 0.0), axis=0, keepdims=True).astype(jnp.int32)
    target = dest_row[...] * CAP + slot
    q = out.shape[0] * CAP
    selector = jnp.where(lax.broadcasted_iota(jnp.int32, (q, n), 0) == target, 1.0, 0.0).astype(BF16)
    height = fluid.shape[0]
    picked = jnp.where(lax.broadcasted_iota(jnp.int32, (height, n), 0) == rows[...], 1.0, 0.0)
    chosen = lax.dot_general(
        selector, picked.astype(BF16), (((1,), (1,)), ((), ())), preferred_element_type=F32
    ).astype(BF16)
    value = fluid[...]
    high = value.astype(BF16)
    rest = value - high.astype(F32)
    mid = rest.astype(BF16)
    low = (rest - mid.astype(F32)).astype(BF16)
    value = mul(chosen, high) + (mul(chosen, mid) + mul(chosen, low))
    out[...] = value.reshape(out.shape)


def turn_kernel(place, struct, fluid, own_s, send_s, own_f, send_f, held_s, held_f):
    core = place[3]
    held_s[...] = struct[...].T.reshape(held_s.shape)
    held_f[...] = fluid[...].T.reshape(held_f.shape)
    own_s[...] = held_s[:, core]
    send_s[...] = held_s[:, 1 - core]
    own_f[...] = held_f[:, core]
    send_f[...] = held_f[:, 1 - core]


def wet_kernel(coupling, received, out):
    right = received[...].reshape(coupling.shape[1], R)
    out[...] = product(parts(coupling[...]), parts(right))


def gathered(tiles, cols, total, at):
    total[:, at : at + TILE * tiles.shape[0]] = jnp.zeros(
        (total.shape[0], TILE * tiles.shape[0], TILE), F32
    )
    for i in range(tiles.shape[0]):
        rows = pl.ds(at + i * TILE, TILE)
        for k in range(tiles.shape[1]):
            c = cols[i, k]
            total[c, rows] = total[c, rows] + tiles[i, k]


def image(total, pieces):
    acc = None
    c = 0
    for piece in pieces:
        n = piece.shape[0] // TILE
        left = jnp.concatenate([total[c + i] for i in range(n)], axis=1) if n > 1 else total[c]
        term = product(parts(left), parts(piece))
        acc = term if acc is None else acc + term
        c += n
    return acc


def fluid_kernel(cols, stiff, mass, lo, own, hi, after, out, total):
    gathered(stiff, cols, total, 0)
    gathered(mass, cols, total, TILE)
    out[...] = image(total, (lo[...], own[...], hi[...])).reshape(out.shape)


def struct_kernel(cols, stiff, mass, lo, own, hi, after, out, total):
    gathered(stiff, cols, total, 0)
    gathered(mass, cols, total, 2 * TILE)
    out[...] = image(total, (lo[...], own[...], hi[...])).reshape(out.shape)


def joined(one, two):
    return jnp.concatenate([one[...].reshape(R // 2, -1), two[...].reshape(R // 2, -1)], axis=1)


def multiply(held, left, one, two):
    right = jnp.concatenate([one, two], axis=0)
    held[...] = product((left[0][...], left[1][...]), parts(right)).reshape(held.shape)


def along_x(place, held, rows, outs):
    for o, out in enumerate(outs):
        d = lax.rem(place[0] + o, 4)
        for h in range(2):
            out[0, h] = held[h * 4 + d, rows, :]


def along_y(place, held, rows, outs):
    for o, out in enumerate(outs):
        d = lax.rem(place[1] + o, 4)
        out[0] = held[:, rows, pl.ds(pl.multiple_of(d * 256, 256), 256)]


def along_z(place, held, outs):
    for o, out in enumerate(outs):
        d = lax.rem(place[2] + o, 4)
        for y in range(4):
            lanes = pl.ds(pl.multiple_of(y * 256 + lax.rem(d, 2) * 128, 128), 128)
            out[:, :, y * 128 : (y + 1) * 128] = held[pl.ds(d // 2 * 4, 4), :, lanes]


def fluid_product_kernel(place, lf0, lf1, if0, if1, o0, o1, o2, o3, fh, fl, held):
    @pl.when(pl.program_id(0) == 0)
    def _():
        fh[...], fl[...] = parts(joined(lf0, lf1))

    multiply(held, (fh, fl), if0[0], if1[0])
    along_x(place, held, slice(0, 64), (o0, o1, o2, o3))


def wet_product_kernel(place, ls0, ls1, ic0, ic1, o0, o1, o2, o3, sh, sl, held):
    sh[...], sl[...] = parts(joined(ls0, ls1))
    multiply(held, (sh, sl), ic0[...], ic1[...])
    along_z(place, held, (o0, o1, o2, o3))


def second_kernel(place, ls0, ls1, is0, is1, *rest):
    outs, (sh, sl, held) = rest[:8], rest[8:]

    @pl.when(pl.program_id(0) == 0)
    def _():
        sh[...], sl[...] = parts(joined(ls0, ls1))

    multiply(held, (sh, sl), is0[0], is1[0])
    along_x(place, held, slice(0, NX), outs[:4])
    along_y(place, held, slice(NX, 64), outs[4:])


def to_y_kernel(place, a0, a1, a2, a3, o0, o1, o2, o3, held):
    held[...] = (a0[...] + a1[...]) + (a2[...] + a3[...])
    for o, out in enumerate((o0, o1, o2, o3)):
        d = lax.rem(place[1] + o, 4)
        out[...] = held[..., pl.ds(pl.multiple_of(d * 256, 256), 256)]


def to_x_kernel(place, a0, a1, a2, a3, b0, b1, b2, b3, o0, o1, o2, o3, held, wet):
    held[...] = (a0[...] + a1[...]) + (a2[...] + a3[...])
    wet[...] = (b0[...] + b1[...]) + (b2[...] + b3[...])
    for o, out in enumerate((o0, o1, o2, o3)):
        d = lax.rem(place[0] + o, 4)
        for m in range(2):
            for h in range(2):
                at = (m * 2 + h) * NY
                out[at : at + NY] = held[m, h * 4 + d]
        for k in range(2):
            at = 4 * NY + k * 64
            out[at : at + 64] = wet[d, :, k * 256 : (k + 1) * 256]


def spread_kernel(place, *refs):
    f, x, y, outs, held, wet = refs[0:4], refs[4:8], refs[8:12], refs[12:20], refs[20], refs[21]
    held[0:2] = (f[0][...] + f[1][...]) + (f[2][...] + f[3][...])
    held[2:4, :, 0:NX] = (x[0][...] + x[1][...]) + (x[2][...] + x[3][...])
    for m in range(2):
        for h in range(2):
            rows = slice((m * 2 + h) * NY, (m * 2 + h + 1) * NY)
            held[2 + m, h, NX:] = (y[0][rows] + y[1][rows]) + (y[2][rows] + y[3][rows])
    for k in range(2):
        rows = slice(4 * NY + k * 64, 4 * NY + (k + 1) * 64)
        wet[k] = (y[0][rows] + y[1][rows]) + (y[2][rows] + y[3][rows])
    for o in range(4):
        d = lax.rem(place[2] + o, 4)
        lanes = pl.ds(pl.multiple_of(lax.rem(d, 2) * 128, 128), 128)
        outs[o][...] = held[:, d // 2, :, lanes]
        d = lax.rem(place[1] + o, 4)
        lanes = pl.ds(pl.multiple_of(lax.rem(d, 2) * 128, 128), 128)
        outs[4 + o][...] = wet[d // 2, :, lanes]


def last_kernel(a0, a1, a2, a3, w0, w1, w2, w3, fstiff, fmass, stiff, mass, wet):
    for m, out in enumerate((fstiff, fmass, stiff, mass)):
        out[...] = (a0[m] + a1[m]) + (a2[m] + a3[m])
    wet[...] = (w0[...] + w1[...]) + (w2[...] + w3[...])


def call(kernel, out, count, smem=0, anywhere=0, scratch=(), flops=0, moved=0):
    run = pl.pallas_call(
        kernel,
        out_shape=out,
        in_specs=[SMEM] * smem + [VMEM] * (count - smem - anywhere) + [ANY] * anywhere,
        out_specs=jax.tree.map(lambda _: VMEM, out),
        scratch_shapes=list(scratch),
        compiler_params=PARAMS,
        cost_estimate=pl.CostEstimate(flops=flops, bytes_accessed=moved, transcendentals=0),
    )
    return run


def exchanged(slots, axis):
    return [slots[0]] + [shifted(slots[o], axis, o) for o in range(1, 4)]


def split(kernel, place, arrived, out, *held):
    size = sum(a.size for a in arrived)
    return call(
        kernel,
        [shape(*out)] * 4,
        1 + len(arrived),
        smem=1,
        scratch=[pltpu.VMEM(dims, F32) for dims in held],
        flops=size,
        moved=5 * size,
    )(place, *arrived)


def spread(place, *arrived):
    return call(
        spread_kernel,
        [shape(4, 64, 128)] * 4 + [shape(64, 128)] * 4,
        13,
        smem=1,
        scratch=[pltpu.VMEM((4, 2, 64, 256), F32), pltpu.VMEM((2, 64, 256), F32)],
        flops=2**20,
        moved=2**22,
    )(place, *arrived)


def partial_sums(kernel, steps, place, lefts, depth, operands, specs, x_rows, y_rows):
    left = pltpu.VMEM((512, depth), BF16)
    outs = [(2, x_rows, R)] * 4 * (x_rows > 0) + [(8, y_rows, 256)] * 4 * (y_rows > 0)
    run = pl.pallas_call(
        kernel,
        grid=(steps,),
        out_shape=[shape(steps, *dims) for dims in outs],
        in_specs=[SMEM] + [VMEM] * len(lefts) + specs,
        out_specs=[pl.BlockSpec((1, *dims), lambda m: (m, 0, 0, 0)) for dims in outs],
        scratch_shapes=[left, left, pltpu.VMEM((8, 64, R), F32)],
        compiler_params=PARAMS,
        cost_estimate=pl.CostEstimate(
            flops=6 * steps * 512 * depth * R, bytes_accessed=4 * steps * 2**20, transcendentals=0
        ),
    )
    return run(place, *lefts, *operands)


def compute(
    struct_basis,
    fluid_basis,
    stiff_tiles,
    mass_tiles,
    fluid_stiff_tiles,
    fluid_mass_tiles,
    struct_cols,
    fluid_cols,
    wet_rows,
    wet_dest,
    coupling,
):
    place = jnp.stack([lax.axis_index(X), lax.axis_index(Y), lax.axis_index(Z), lax.axis_index("core")]).astype(
        jnp.int32
    )
    below_s = from_behind(struct_basis[-TILE:], 1)
    above_s = from_behind(struct_basis[:TILE], -1)
    below_f = from_behind(fluid_basis, 1)
    above_f = from_behind(fluid_basis, -1)

    outgoing = call(route_kernel, shape(128, CAP, R), 3, flops=2 * 3 * 256 * 128 * R, moved=2**21)(
        wet_dest.reshape(1, -1), wet_rows.reshape(1, -1), fluid_basis
    )
    received = lax.all_to_all(outgoing, AXES, split_axis=0, concat_axis=0, tiled=True)

    own_s, send_s, own_f, send_f = call(
        turn_kernel,
        [shape(8, 64, 256)] * 2 + [shape(8, 64, 128)] * 2,
        3,
        smem=1,
        scratch=[pltpu.VMEM((8, 2, 64, 256), F32), pltpu.VMEM((8, 2, 64, 128), F32)],
        flops=2**20,
        moved=3 * 2**20,
    )(place, struct_basis, fluid_basis)
    left_s = shifted(send_s, "core", 1)
    left_f = shifted(send_f, "core", 1)

    image_c = call(wet_kernel, shape(256, R), 2, flops=6 * 256 * 256 * R, moved=2**21)(coupling, received)
    other_c = shifted(image_c, "core", 1)

    image_f = call(
        fluid_kernel,
        shape(2, 128, R),
        7,
        smem=1,
        anywhere=1,
        scratch=[pltpu.VMEM((3, 256, TILE), F32)],
        flops=6 * 256 * 384 * R,
        moved=3 * 2**20,
    )(fluid_cols, fluid_stiff_tiles, fluid_mass_tiles, below_f, fluid_basis, above_f, own_s)
    other_f = shifted(image_f, "core", 1)

    def block(rows):
        return pl.BlockSpec((1, rows, R), lambda m: (m, 0, 0))

    fluid = partial_sums(
        fluid_product_kernel, 2, place, (own_f, left_f), 256, (image_f, other_f), [block(128)] * 2, 64, 0
    )
    fluid_x = exchanged(fluid, X)

    image_s = call(
        struct_kernel,
        shape(2, 256, R),
        7,
        smem=1,
        anywhere=1,
        scratch=[pltpu.VMEM((4, 512, TILE), F32)],
        flops=6 * 512 * 512 * R,
        moved=5 * 2**20,
    )(struct_cols, stiff_tiles, mass_tiles, below_s, struct_basis, above_s, fluid[0])
    other_s = shifted(image_s, "core", 1)

    coupled = call(
        wet_product_kernel,
        [shape(4, 64, 512)] * 4,
        5,
        smem=1,
        scratch=[pltpu.VMEM((512, 512), BF16)] * 2 + [pltpu.VMEM((8, 64, R), F32)],
        flops=6 * 512 * 512 * R,
        moved=5 * 2**20,
    )(place, own_s, left_s, image_c, other_c)
    coupled_z = exchanged(coupled, Z)
    struct = partial_sums(second_kernel, 2, place, (own_s, left_s), 512, (image_s, other_s), [block(256)] * 2, NX, NY)
    struct_x = exchanged(struct[0:4], X)
    struct_y = exchanged(struct[4:8], Y)

    fluid_xy = exchanged(split(to_y_kernel, place, fluid_x, (2, 2, 64, 256), (2, 2, 64, R)), Y)
    struct_xy = exchanged(split(to_y_kernel, place, struct_x, (2, 2, NX, 256), (2, 2, NX, R)), Y)
    both_x = exchanged(
        split(to_x_kernel, place, struct_y + coupled_z, (4 * NY + 128, 256), (2, 8, NY, 256), (4, 64, 512)), X
    )
    parted = spread(place, *fluid_xy, *struct_xy, *both_x)
    summed = exchanged(parted[:4], Z) + exchanged(parted[4:], Y)
    fstiff, fmass, stiff, mass, wet = call(last_kernel, [shape(64, 128)] * 5, 8, flops=2**18, moved=2**20)(*summed)
    return stiff, mass, fstiff, fmass, wet


def solution(mesh):
    fine = Mesh(mesh.devices.reshape(2, 4, 2, 4, 2), AXES)
    return jax.shard_map(
        compute,
        mesh=fine,
        in_specs=(
            P(AXES, None),
            P(AXES, None),
            P(AXES, None, None, None),
            P(AXES, None, None, None),
            P(AXES, None, None, None),
            P(AXES, None, None, None),
            P(AXES, None),
            P(AXES, None),
            P(AXES),
            P(AXES, None),
            P(AXES, None),
        ),
        out_specs=(P(ROW, COL),) * 5,
        check_vma=False,
    )
```

```python
import functools

import jax
import jax.numpy as jnp
from jax import lax
from jax.experimental import pallas as pl
from jax.experimental.pallas import tpu as pltpu
from jax.sharding import Mesh
from jax.sharding import PartitionSpec as P


R = 1024
TILE = 128
CAP = 2
F32 = jnp.float32
BF16 = jnp.bfloat16

AXES = ("zhi", "x", "core", "y", "zlo")
ROW = ("zhi", "x", "core")
COL = ("y", "zlo")
X, Y, Z = "x", "y", ("zhi", "zlo")
YZ, XZ = ("y", "zhi", "zlo"), ("x", "zhi", "zlo")
HALF = 32


VMEM = pl.BlockSpec(memory_space=pltpu.VMEM)
SMEM = pl.BlockSpec(memory_space=pltpu.SMEM)
ANY = pl.BlockSpec(memory_space=pl.ANY)
PARAMS = pltpu.CompilerParams(vmem_limit_bytes=60 * 1024 * 1024)


def shape(*dims):
    return jax.ShapeDtypeStruct(dims, F32)


def parts(value):
    high = value.astype(BF16)
    low = (value - high.astype(F32)).astype(BF16)
    return high, low


def mul(a, b):
    return jnp.dot(a, b, preferred_element_type=F32)


def product(a, b):
    ah, al = a
    bh, bl = b
    return mul(ah, bh) + (mul(ah, bl) + mul(al, bh))


def shifted(value, axis, by):
    size = lax.axis_size(axis)
    return lax.ppermute(value, axis, [(i, (i + by) % size) for i in range(size)])


def from_behind(value, by):
    size = lax.axis_size(AXES)
    pairs = [(i, i + by) for i in range(size) if 0 <= i + by < size]
    return lax.ppermute(value, AXES, pairs)


def route_kernel(dest_row, rows, fluid, out):
    n = dest_row.shape[1]
    dest = jnp.broadcast_to(dest_row[...].astype(F32), (n, n))
    earlier = lax.broadcasted_iota(jnp.int32, (n, n), 0) < lax.broadcasted_iota(jnp.int32, (n, n), 1)
    same = (dest.T == dest) & earlier
    slot = jnp.sum(jnp.where(same, 1.0, 0.0), axis=0, keepdims=True).astype(jnp.int32)
    target = dest_row[...] * CAP + slot
    q = out.shape[0] * CAP
    selector = jnp.where(lax.broadcasted_iota(jnp.int32, (q, n), 0) == target, 1.0, 0.0).astype(BF16)
    height = fluid.shape[0]
    picked = jnp.where(lax.broadcasted_iota(jnp.int32, (height, n), 0) == rows[...], 1.0, 0.0)
    chosen = lax.dot_general(
        selector, picked.astype(BF16), (((1,), (1,)), ((), ())), preferred_element_type=F32
    ).astype(BF16)
    value = fluid[...]
    high = value.astype(BF16)
    rest = value - high.astype(F32)
    mid = rest.astype(BF16)
    low = (rest - mid.astype(F32)).astype(BF16)
    value = mul(chosen, high) + (mul(chosen, mid) + mul(chosen, low))
    out[...] = value.reshape(out.shape)


def turn_kernel(place, struct, fluid, own_s, send_s, own_f, send_f, held_s, held_f):
    core = place[3]
    held_s[...] = struct[...].T.reshape(held_s.shape)
    held_f[...] = fluid[...].T.reshape(held_f.shape)
    own_s[...] = held_s[:, core]
    send_s[...] = held_s[:, 1 - core]
    own_f[...] = held_f[:, core]
    send_f[...] = held_f[:, 1 - core]


def wet_kernel(coupling, received, out):
    right = received[...].reshape(coupling.shape[1], R)
    out[...] = product(parts(coupling[...]), parts(right))


def gathered(tiles, cols, total, at):
    total[:, at : at + TILE * tiles.shape[0]] = jnp.zeros(
        (total.shape[0], TILE * tiles.shape[0], TILE), F32
    )
    for i in range(tiles.shape[0]):
        rows = pl.ds(at + i * TILE, TILE)
        for k in range(tiles.shape[1]):
            c = cols[i, k]
            total[c, rows] = total[c, rows] + tiles[i, k]


def image(total, pieces):
    acc = None
    c = 0
    for piece in pieces:
        n = piece.shape[0] // TILE
        left = jnp.concatenate([total[c + i] for i in range(n)], axis=1) if n > 1 else total[c]
        term = product(parts(left), parts(piece))
        acc = term if acc is None else acc + term
        c += n
    return acc


def fluid_kernel(cols, stiff, mass, lo, own, hi, after, out, total):
    gathered(stiff, cols, total, 0)
    gathered(mass, cols, total, TILE)
    out[...] = image(total, (lo[...], own[...], hi[...])).reshape(out.shape)


def struct_kernel(cols, stiff, mass, lo, own, hi, after, out, total):
    gathered(stiff, cols, total, 0)
    gathered(mass, cols, total, 2 * TILE)
    out[...] = image(total, (lo[...], own[...], hi[...])).reshape(out.shape)


def joined(one, two):
    return jnp.concatenate([one[...].reshape(R // 2, -1), two[...].reshape(R // 2, -1)], axis=1)


def multiply(held, left, one, two):
    right = jnp.concatenate([one, two], axis=0)
    held[...] = product((left[0][...], left[1][...]), parts(right)).reshape(held.shape)


def send_off(place, held, outs):
    for o in range(4):
        dx = lax.rem(place[0] + o, 4)
        dy = lax.rem(place[1] + o, 4)
        for h in range(2):
            outs[o][0, h] = held[h * 4 + dx, 0:HALF, :]
        outs[4 + o][0] = held[:, HALF:, pl.ds(pl.multiple_of(dy * 256, 256), 256)]


def fluid_product_kernel(place, lf0, lf1, if0, if1, *rest):
    outs, (fh, fl, held) = rest[:8], rest[8:]

    @pl.when(pl.program_id(0) == 0)
    def _():
        fh[...], fl[...] = parts(joined(lf0, lf1))

    multiply(held, (fh, fl), if0[0], if1[0])
    send_off(place, held, outs)


def wet_product_kernel(place, ls0, ls1, ic0, ic1, *rest):
    outs, (sh, sl, held) = rest[8:16], rest[16:]
    sh[...], sl[...] = parts(joined(ls0, ls1))
    multiply(held, (sh, sl), ic0[...], ic1[...])
    send_off(place, held, outs)


def second_kernel(place, ls0, ls1, is0, is1, *rest):
    outs, (sh, sl, held) = rest[:8], rest[8:]

    @pl.when(pl.program_id(0) == 0)
    def _():
        sh[...], sl[...] = parts(joined(ls0, ls1))

    multiply(held, (sh, sl), is0[0], is1[0])
    send_off(place, held, outs)


def split_kernel(axis, place, a0, a1, a2, a3, o0, o1, o2, o3, held):
    held[...] = (a0[...] + a1[...]) + (a2[...] + a3[...])
    for o, out in enumerate((o0, o1, o2, o3)):
        d = lax.rem(place[axis] + o, 4)
        if axis == 1:
            out[...] = held[..., pl.ds(pl.multiple_of(d * 256, 256), 256)]
        else:
            for h in range(2):
                out[:, h] = held[:, h * 4 + d]


def spread_kernel(place, x0, x1, x2, x3, y0, y1, y2, y3, o0, o1, o2, o3, held):
    held[:, :, 0:HALF] = (x0[...] + x1[...]) + (x2[...] + x3[...])
    held[:, :, HALF:] = (y0[...] + y1[...]) + (y2[...] + y3[...])
    for o, out in enumerate((o0, o1, o2, o3)):
        d = lax.rem(place[2] + o, 4)
        lanes = pl.ds(pl.multiple_of(lax.rem(d, 2) * 128, 128), 128)
        out[...] = held[:, d // 2, :, lanes]


def plane_x_kernel(a0, a1, a2, a3, out, held):
    held[...] = (a0[...] + a1[...]) + (a2[...] + a3[...])
    for y in range(4):
        for h in range(2):
            for l in range(2):
                at = (y * 2 + l) * 128
                out[y * 4 + h * 2 + l] = held[:, h, :, at : at + 128]


def plane_y_kernel(a0, a1, a2, a3, out, held):
    held[...] = (a0[...] + a1[...]) + (a2[...] + a3[...])
    for x in range(4):
        for h in range(2):
            for l in range(2):
                out[x * 4 + h * 2 + l] = held[:, h * 4 + x, :, l * 128 : (l + 1) * 128]


def last_kernel(a0, a1, a2, a3, *outs):
    for m, out in enumerate(outs):
        out[...] = (a0[m] + a1[m]) + (a2[m] + a3[m])


def last_plane_kernel(top, low, *outs):
    for m, out in enumerate(outs):
        for ref, at in ((top, 0), (low, HALF)):
            terms = [ref[i, m] for i in range(ref.shape[0])]
            while len(terms) > 1:
                terms = [terms[i] + terms[i + 1] for i in range(0, len(terms), 2)]
            out[at : at + HALF] = terms[0]


def call(kernel, out, count, smem=0, anywhere=0, scratch=(), flops=0, moved=0):
    run = pl.pallas_call(
        kernel,
        out_shape=out,
        in_specs=[SMEM] * smem + [VMEM] * (count - smem - anywhere) + [ANY] * anywhere,
        out_specs=jax.tree.map(lambda _: VMEM, out),
        scratch_shapes=list(scratch),
        compiler_params=PARAMS,
        cost_estimate=pl.CostEstimate(flops=flops, bytes_accessed=moved, transcendentals=0),
    )
    return run


def exchanged(slots, axis):
    return [slots[0]] + [shifted(slots[o], axis, o) for o in range(1, 4)]


def split(place, arrived, axis):
    count = arrived[0].shape[0]
    size = arrived[0].size
    return call(
        functools.partial(split_kernel, axis),
        [shape(count, 2, HALF, 256)] * 4,
        5,
        smem=1,
        scratch=[pltpu.VMEM(arrived[0].shape, F32)],
        flops=3 * size,
        moved=20 * size,
    )(place, *arrived)


def plane(kernel, arrived, axes):
    size = arrived[0].size
    slots = call(
        kernel,
        shape(16, arrived[0].shape[0], HALF, 128),
        4,
        scratch=[pltpu.VMEM(arrived[0].shape, F32)],
        flops=3 * size,
        moved=20 * size,
    )(*arrived)
    return lax.all_to_all(slots, axes, split_axis=0, concat_axis=0, tiled=True)


def spread(place, x, y):
    count = x[0].shape[0]
    return call(
        spread_kernel,
        [shape(count, 64, 128)] * 4,
        9,
        smem=1,
        scratch=[pltpu.VMEM((count, 2, 64, 256), F32)],
        flops=6 * x[0].size,
        moved=40 * x[0].size,
    )(place, *x, *y)


def partial_sums(kernel, steps, at, count, place, lefts, depth, operands, specs, carried=()):
    left = pltpu.VMEM((512, depth), BF16)
    run = pl.pallas_call(
        kernel,
        grid=(steps,),
        out_shape=[shape(count, 2, HALF, R)] * 4 + [shape(count, 8, HALF, 256)] * 4,
        in_specs=[SMEM] + [VMEM] * len(lefts) + specs + [ANY] * len(carried),
        out_specs=[pl.BlockSpec((1, 2, HALF, R), lambda m: (m + at, 0, 0, 0))] * 4
        + [pl.BlockSpec((1, 8, HALF, 256), lambda m: (m + at, 0, 0, 0))] * 4,
        scratch_shapes=[left, left, pltpu.VMEM((8, 64, R), F32)],
        input_output_aliases={1 + len(lefts) + len(specs) + i: i for i in range(len(carried))},
        compiler_params=PARAMS,
        cost_estimate=pl.CostEstimate(
            flops=6 * steps * 512 * depth * R, bytes_accessed=4 * steps * 2**20, transcendentals=0
        ),
    )
    return run(place, *lefts, *operands, *carried)


def compute(
    struct_basis,
    fluid_basis,
    stiff_tiles,
    mass_tiles,
    fluid_stiff_tiles,
    fluid_mass_tiles,
    struct_cols,
    fluid_cols,
    wet_rows,
    wet_dest,
    coupling,
):
    place = jnp.stack([lax.axis_index(X), lax.axis_index(Y), lax.axis_index(Z), lax.axis_index("core")]).astype(
        jnp.int32
    )
    below_s = from_behind(struct_basis[-TILE:], 1)
    above_s = from_behind(struct_basis[:TILE], -1)
    below_f = from_behind(fluid_basis, 1)
    above_f = from_behind(fluid_basis, -1)

    outgoing = call(route_kernel, shape(128, CAP, R), 3, flops=2 * 3 * 256 * 128 * R, moved=2**21)(
        wet_dest.reshape(1, -1), wet_rows.reshape(1, -1), fluid_basis
    )
    received = lax.all_to_all(outgoing, AXES, split_axis=0, concat_axis=0, tiled=True)

    own_s, send_s, own_f, send_f = call(
        turn_kernel,
        [shape(8, 64, 256)] * 2 + [shape(8, 64, 128)] * 2,
        3,
        smem=1,
        scratch=[pltpu.VMEM((8, 2, 64, 256), F32), pltpu.VMEM((8, 2, 64, 128), F32)],
        flops=2**20,
        moved=3 * 2**20,
    )(place, struct_basis, fluid_basis)
    left_s = shifted(send_s, "core", 1)
    left_f = shifted(send_f, "core", 1)

    image_c = call(wet_kernel, shape(256, R), 2, flops=6 * 256 * 256 * R, moved=2**21)(coupling, received)
    other_c = shifted(image_c, "core", 1)

    image_f = call(
        fluid_kernel,
        shape(2, 128, R),
        7,
        smem=1,
        anywhere=1,
        scratch=[pltpu.VMEM((3, 256, TILE), F32)],
        flops=6 * 256 * 384 * R,
        moved=3 * 2**20,
    )(fluid_cols, fluid_stiff_tiles, fluid_mass_tiles, below_f, fluid_basis, above_f, own_s)
    other_f = shifted(image_f, "core", 1)

    def block(rows):
        return pl.BlockSpec((1, rows, R), lambda m: (m, 0, 0))

    fluid = partial_sums(
        fluid_product_kernel, 2, 0, 3, place, (own_f, left_f), 256, (image_f, other_f), [block(128)] * 2
    )
    first = partial_sums(
        wet_product_kernel, 1, 2, 3, place, (own_s, left_s), 512, (image_c, other_c), [VMEM] * 2, fluid
    )
    first_x = exchanged(first[0:4], X)
    first_y = exchanged(first[4:8], Y)

    image_s = call(
        struct_kernel,
        shape(2, 256, R),
        7,
        smem=1,
        anywhere=1,
        scratch=[pltpu.VMEM((4, 512, TILE), F32)],
        flops=6 * 512 * 512 * R,
        moved=5 * 2**20,
    )(struct_cols, stiff_tiles, mass_tiles, below_s, struct_basis, above_s, first[0])
    other_s = shifted(image_s, "core", 1)

    second = partial_sums(second_kernel, 2, 0, 2, place, (own_s, left_s), 512, (image_s, other_s), [block(256)] * 2)
    second_x = exchanged(second[0:4], X)
    second_y = exchanged(second[4:8], Y)

    first_xy = exchanged(split(place, first_x, 1), Y)
    first_yx = exchanged(split(place, first_y, 0), X)
    first_z = exchanged(spread(place, first_xy, first_yx), Z)
    second_top = plane(plane_x_kernel, second_x, YZ)
    second_low = plane(plane_y_kernel, second_y, XZ)
    fstiff, fmass, wet = call(last_kernel, [shape(64, 128)] * 3, 4, flops=2**17, moved=2**19)(*first_z)
    stiff, mass = call(last_plane_kernel, [shape(64, 128)] * 2, 2, flops=2**18, moved=2**20)(second_top, second_low)
    return stiff, mass, fstiff, fmass, wet


def solution(mesh):
    fine = Mesh(mesh.devices.reshape(2, 4, 2, 4, 2), AXES)
    return jax.shard_map(
        compute,
        mesh=fine,
        in_specs=(
            P(AXES, None),
            P(AXES, None),
            P(AXES, None, None, None),
            P(AXES, None, None, None),
            P(AXES, None, None, None),
            P(AXES, None, None, None),
            P(AXES, None),
            P(AXES, None),
            P(AXES),
            P(AXES, None),
            P(AXES, None),
        ),
        out_specs=(P(ROW, COL),) * 5,
        check_vma=False,
    )
```

```python
import functools

import jax
import jax.numpy as jnp
from jax import lax
from jax.experimental import pallas as pl
from jax.experimental.pallas import tpu as pltpu
from jax.sharding import Mesh
from jax.sharding import PartitionSpec as P


R = 1024
TILE = 128
CAP = 2
F32 = jnp.float32
BF16 = jnp.bfloat16

AXES = ("zhi", "x", "core", "y", "zlo")
ROW = ("zhi", "x", "core")
COL = ("y", "zlo")
X, Y, Z = "x", "y", ("zhi", "zlo")
HALF = 32


VMEM = pl.BlockSpec(memory_space=pltpu.VMEM)
SMEM = pl.BlockSpec(memory_space=pltpu.SMEM)
ANY = pl.BlockSpec(memory_space=pl.ANY)
PARAMS = pltpu.CompilerParams(vmem_limit_bytes=60 * 1024 * 1024)


def shape(*dims):
    return jax.ShapeDtypeStruct(dims, F32)


def parts(value):
    high = value.astype(BF16)
    low = (value - high.astype(F32)).astype(BF16)
    return high, low


def mul(a, b):
    return jnp.dot(a, b, preferred_element_type=F32)


def product(a, b):
    ah, al = a
    bh, bl = b
    return mul(ah, bh) + (mul(ah, bl) + mul(al, bh))


def shifted(value, axis, by):
    size = lax.axis_size(axis)
    return lax.ppermute(value, axis, [(i, (i + by) % size) for i in range(size)])


def from_behind(value, by):
    size = lax.axis_size(AXES)
    pairs = [(i, i + by) for i in range(size) if 0 <= i + by < size]
    return lax.ppermute(value, AXES, pairs)


def route_kernel(dest_row, rows, fluid, out):
    n = dest_row.shape[1]
    dest = jnp.broadcast_to(dest_row[...].astype(F32), (n, n))
    earlier = lax.broadcasted_iota(jnp.int32, (n, n), 0) < lax.broadcasted_iota(jnp.int32, (n, n), 1)
    same = (dest.T == dest) & earlier
    slot = jnp.sum(jnp.where(same, 1.0, 0.0), axis=0, keepdims=True).astype(jnp.int32)
    target = dest_row[...] * CAP + slot
    q = out.shape[0] * CAP
    selector = jnp.where(lax.broadcasted_iota(jnp.int32, (q, n), 0) == target, 1.0, 0.0).astype(BF16)
    height = fluid.shape[0]
    picked = jnp.where(lax.broadcasted_iota(jnp.int32, (height, n), 0) == rows[...], 1.0, 0.0)
    chosen = lax.dot_general(
        selector, picked.astype(BF16), (((1,), (1,)), ((), ())), preferred_element_type=F32
    ).astype(BF16)
    value = fluid[...]
    high = value.astype(BF16)
    rest = value - high.astype(F32)
    mid = rest.astype(BF16)
    low = (rest - mid.astype(F32)).astype(BF16)
    value = mul(chosen, high) + (mul(chosen, mid) + mul(chosen, low))
    out[...] = value.reshape(out.shape)


def turn_kernel(place, struct, fluid, own_s, send_s, own_f, send_f, held_s, held_f):
    core = place[3]
    held_s[...] = struct[...].T.reshape(held_s.shape)
    held_f[...] = fluid[...].T.reshape(held_f.shape)
    own_s[...] = held_s[:, core]
    send_s[...] = held_s[:, 1 - core]
    own_f[...] = held_f[:, core]
    send_f[...] = held_f[:, 1 - core]


def wet_kernel(coupling, received, out):
    right = received[...].reshape(coupling.shape[1], R)
    out[...] = product(parts(coupling[...]), parts(right))


def gathered(tiles, cols, total, at):
    total[:, at : at + TILE * tiles.shape[0]] = jnp.zeros(
        (total.shape[0], TILE * tiles.shape[0], TILE), F32
    )
    for i in range(tiles.shape[0]):
        rows = pl.ds(at + i * TILE, TILE)
        for k in range(tiles.shape[1]):
            c = cols[i, k]
            total[c, rows] = total[c, rows] + tiles[i, k]


def image(total, pieces):
    acc = None
    c = 0
    for piece in pieces:
        n = piece.shape[0] // TILE
        left = jnp.concatenate([total[c + i] for i in range(n)], axis=1) if n > 1 else total[c]
        term = product(parts(left), parts(piece))
        acc = term if acc is None else acc + term
        c += n
    return acc


def fluid_kernel(cols, stiff, mass, lo, own, hi, after, out, total):
    gathered(stiff, cols, total, 0)
    gathered(mass, cols, total, TILE)
    out[...] = image(total, (lo[...], own[...], hi[...])).reshape(out.shape)


def struct_kernel(cols, stiff, mass, lo, own, hi, after, out, total):
    gathered(stiff, cols, total, 0)
    gathered(mass, cols, total, 2 * TILE)
    out[...] = image(total, (lo[...], own[...], hi[...])).reshape(out.shape)


def joined(one, two):
    return jnp.concatenate([one[...].reshape(R // 2, -1), two[...].reshape(R // 2, -1)], axis=1)


def multiply(held, left, one, two):
    right = jnp.concatenate([one, two], axis=0)
    held[...] = product((left[0][...], left[1][...]), parts(right)).reshape(held.shape)


def send_off(place, held, outs):
    for o in range(4):
        dx = lax.rem(place[0] + o, 4)
        dy = lax.rem(place[1] + o, 4)
        for h in range(2):
            outs[o][0, h] = held[h * 4 + dx, 0:HALF, :]
        outs[4 + o][0] = held[:, HALF:, pl.ds(pl.multiple_of(dy * 256, 256), 256)]


def fluid_product_kernel(place, lf0, lf1, if0, if1, *rest):
    outs, (fh, fl, held) = rest[:8], rest[8:]

    @pl.when(pl.program_id(0) == 0)
    def _():
        fh[...], fl[...] = parts(joined(lf0, lf1))

    multiply(held, (fh, fl), if0[0], if1[0])
    send_off(place, held, outs)


def wet_product_kernel(place, ls0, ls1, ic0, ic1, *rest):
    outs, (sh, sl, held) = rest[8:16], rest[16:]
    sh[...], sl[...] = parts(joined(ls0, ls1))
    multiply(held, (sh, sl), ic0[...], ic1[...])
    send_off(place, held, outs)


def second_kernel(place, ls0, ls1, is0, is1, *rest):
    outs, (sh, sl, held) = rest[:8], rest[8:]

    @pl.when(pl.program_id(0) == 0)
    def _():
        sh[...], sl[...] = parts(joined(ls0, ls1))

    multiply(held, (sh, sl), is0[0], is1[0])
    send_off(place, held, outs)


def split_kernel(axis, place, a0, a1, a2, a3, o0, o1, o2, o3, held):
    held[...] = (a0[...] + a1[...]) + (a2[...] + a3[...])
    for o, out in enumerate((o0, o1, o2, o3)):
        d = lax.rem(place[axis] + o, 4)
        if axis == 1:
            out[...] = held[..., pl.ds(pl.multiple_of(d * 256, 256), 256)]
        else:
            for h in range(2):
                out[:, h] = held[:, h * 4 + d]


def spread_kernel(place, *refs):
    ins, outs, held = refs[:16], refs[16:20], refs[20]
    at = 0
    for x, y in ((ins[0:4], ins[4:8]), (ins[8:12], ins[12:16])):
        rows = slice(at, at + x[0].shape[0])
        held[rows, :, 0:HALF] = (x[0][...] + x[1][...]) + (x[2][...] + x[3][...])
        held[rows, :, HALF:] = (y[0][...] + y[1][...]) + (y[2][...] + y[3][...])
        at = rows.stop
    for o, out in enumerate(outs):
        d = lax.rem(place[2] + o, 4)
        lanes = pl.ds(pl.multiple_of(lax.rem(d, 2) * 128, 128), 128)
        out[...] = held[:, d // 2, :, lanes]


def last_kernel(a0, a1, a2, a3, *outs):
    for m, out in enumerate(outs):
        out[...] = (a0[m] + a1[m]) + (a2[m] + a3[m])


def call(kernel, out, count, smem=0, anywhere=0, scratch=(), flops=0, moved=0):
    run = pl.pallas_call(
        kernel,
        out_shape=out,
        in_specs=[SMEM] * smem + [VMEM] * (count - smem - anywhere) + [ANY] * anywhere,
        out_specs=jax.tree.map(lambda _: VMEM, out),
        scratch_shapes=list(scratch),
        compiler_params=PARAMS,
        cost_estimate=pl.CostEstimate(flops=flops, bytes_accessed=moved, transcendentals=0),
    )
    return run


def exchanged(slots, axis):
    return [slots[0]] + [shifted(slots[o], axis, o) for o in range(1, 4)]


def split(place, arrived, axis):
    count = arrived[0].shape[0]
    size = arrived[0].size
    return call(
        functools.partial(split_kernel, axis),
        [shape(count, 2, HALF, 256)] * 4,
        5,
        smem=1,
        scratch=[pltpu.VMEM(arrived[0].shape, F32)],
        flops=3 * size,
        moved=20 * size,
    )(place, *arrived)


def spread(place, *arrived):
    return call(
        spread_kernel,
        [shape(5, 64, 128)] * 4,
        17,
        smem=1,
        scratch=[pltpu.VMEM((5, 2, 64, 256), F32)],
        flops=2**20,
        moved=2**22,
    )(place, *arrived)


def partial_sums(kernel, steps, at, count, place, lefts, depth, operands, specs, carried=()):
    left = pltpu.VMEM((512, depth), BF16)
    run = pl.pallas_call(
        kernel,
        grid=(steps,),
        out_shape=[shape(count, 2, HALF, R)] * 4 + [shape(count, 8, HALF, 256)] * 4,
        in_specs=[SMEM] + [VMEM] * len(lefts) + specs + [ANY] * len(carried),
        out_specs=[pl.BlockSpec((1, 2, HALF, R), lambda m: (m + at, 0, 0, 0))] * 4
        + [pl.BlockSpec((1, 8, HALF, 256), lambda m: (m + at, 0, 0, 0))] * 4,
        scratch_shapes=[left, left, pltpu.VMEM((8, 64, R), F32)],
        input_output_aliases={1 + len(lefts) + len(specs) + i: i for i in range(len(carried))},
        compiler_params=PARAMS,
        cost_estimate=pl.CostEstimate(
            flops=6 * steps * 512 * depth * R, bytes_accessed=4 * steps * 2**20, transcendentals=0
        ),
    )
    return run(place, *lefts, *operands, *carried)


def compute(
    struct_basis,
    fluid_basis,
    stiff_tiles,
    mass_tiles,
    fluid_stiff_tiles,
    fluid_mass_tiles,
    struct_cols,
    fluid_cols,
    wet_rows,
    wet_dest,
    coupling,
):
    place = jnp.stack([lax.axis_index(X), lax.axis_index(Y), lax.axis_index(Z), lax.axis_index("core")]).astype(
        jnp.int32
    )
    below_s = from_behind(struct_basis[-TILE:], 1)
    above_s = from_behind(struct_basis[:TILE], -1)
    below_f = from_behind(fluid_basis, 1)
    above_f = from_behind(fluid_basis, -1)

    outgoing = call(route_kernel, shape(128, CAP, R), 3, flops=2 * 3 * 256 * 128 * R, moved=2**21)(
        wet_dest.reshape(1, -1), wet_rows.reshape(1, -1), fluid_basis
    )
    received = lax.all_to_all(outgoing, AXES, split_axis=0, concat_axis=0, tiled=True)

    own_s, send_s, own_f, send_f = call(
        turn_kernel,
        [shape(8, 64, 256)] * 2 + [shape(8, 64, 128)] * 2,
        3,
        smem=1,
        scratch=[pltpu.VMEM((8, 2, 64, 256), F32), pltpu.VMEM((8, 2, 64, 128), F32)],
        flops=2**20,
        moved=3 * 2**20,
    )(place, struct_basis, fluid_basis)
    left_s = shifted(send_s, "core", 1)
    left_f = shifted(send_f, "core", 1)

    image_c = call(wet_kernel, shape(256, R), 2, flops=6 * 256 * 256 * R, moved=2**21)(coupling, received)
    other_c = shifted(image_c, "core", 1)

    image_f = call(
        fluid_kernel,
        shape(2, 128, R),
        7,
        smem=1,
        anywhere=1,
        scratch=[pltpu.VMEM((3, 256, TILE), F32)],
        flops=6 * 256 * 384 * R,
        moved=3 * 2**20,
    )(fluid_cols, fluid_stiff_tiles, fluid_mass_tiles, below_f, fluid_basis, above_f, own_s)
    other_f = shifted(image_f, "core", 1)

    def block(rows):
        return pl.BlockSpec((1, rows, R), lambda m: (m, 0, 0))

    fluid = partial_sums(
        fluid_product_kernel, 2, 0, 3, place, (own_f, left_f), 256, (image_f, other_f), [block(128)] * 2
    )
    first = partial_sums(
        wet_product_kernel, 1, 2, 3, place, (own_s, left_s), 512, (image_c, other_c), [VMEM] * 2, fluid
    )
    first_x = exchanged(first[0:4], X)
    first_y = exchanged(first[4:8], Y)

    image_s = call(
        struct_kernel,
        shape(2, 256, R),
        7,
        smem=1,
        anywhere=1,
        scratch=[pltpu.VMEM((4, 512, TILE), F32)],
        flops=6 * 512 * 512 * R,
        moved=5 * 2**20,
    )(struct_cols, stiff_tiles, mass_tiles, below_s, struct_basis, above_s, first[0])
    other_s = shifted(image_s, "core", 1)

    second = partial_sums(second_kernel, 2, 0, 2, place, (own_s, left_s), 512, (image_s, other_s), [block(256)] * 2)
    second_x = exchanged(second[0:4], X)
    second_y = exchanged(second[4:8], Y)

    first_xy = exchanged(split(place, first_x, 1), Y)
    first_yx = exchanged(split(place, first_y, 0), X)
    second_xy = exchanged(split(place, second_x, 1), Y)
    second_yx = exchanged(split(place, second_y, 0), X)
    summed = exchanged(spread(place, *first_xy, *first_yx, *second_xy, *second_yx), Z)
    fstiff, fmass, wet, stiff, mass = call(last_kernel, [shape(64, 128)] * 5, 4, flops=2**18, moved=2**20)(*summed)
    return stiff, mass, fstiff, fmass, wet


def solution(mesh):
    fine = Mesh(mesh.devices.reshape(2, 4, 2, 4, 2), AXES)
    return jax.shard_map(
        compute,
        mesh=fine,
        in_specs=(
            P(AXES, None),
            P(AXES, None),
            P(AXES, None, None, None),
            P(AXES, None, None, None),
            P(AXES, None, None, None),
            P(AXES, None, None, None),
            P(AXES, None),
            P(AXES, None),
            P(AXES),
            P(AXES, None),
            P(AXES, None),
        ),
        out_specs=(P(ROW, COL),) * 5,
        check_vma=False,
    )
```

```python
import functools

import jax
import jax.numpy as jnp
from jax import lax
from jax.experimental import pallas as pl
from jax.experimental.pallas import tpu as pltpu
from jax.sharding import Mesh
from jax.sharding import PartitionSpec as P


R = 1024
TILE = 128
CAP = 2
F32 = jnp.float32
BF16 = jnp.bfloat16

AXES = ("zhi", "x", "core", "y", "zlo")
ROW = ("zhi", "x", "core")
COL = ("y", "zlo")
X, Y, Z = "x", "y", ("zhi", "zlo")
HALF = 32


VMEM = pl.BlockSpec(memory_space=pltpu.VMEM)
SMEM = pl.BlockSpec(memory_space=pltpu.SMEM)
ANY = pl.BlockSpec(memory_space=pl.ANY)
PARAMS = pltpu.CompilerParams(vmem_limit_bytes=60 * 1024 * 1024)


def shape(*dims):
    return jax.ShapeDtypeStruct(dims, F32)


def parts(value):
    high = value.astype(BF16)
    low = (value - high.astype(F32)).astype(BF16)
    return high, low


def mul(a, b):
    return jnp.dot(a, b, preferred_element_type=F32)


def product(a, b):
    ah, al = a
    bh, bl = b
    return mul(ah, bh) + (mul(ah, bl) + mul(al, bh))


def shifted(value, axis, by):
    size = lax.axis_size(axis)
    return lax.ppermute(value, axis, [(i, (i + by) % size) for i in range(size)])


def from_behind(value, by):
    size = lax.axis_size(AXES)
    pairs = [(i, i + by) for i in range(size) if 0 <= i + by < size]
    return lax.ppermute(value, AXES, pairs)


def route_kernel(dest_row, rows, fluid, out):
    n = dest_row.shape[1]
    dest = jnp.broadcast_to(dest_row[...].astype(F32), (n, n))
    earlier = lax.broadcasted_iota(jnp.int32, (n, n), 0) < lax.broadcasted_iota(jnp.int32, (n, n), 1)
    same = (dest.T == dest) & earlier
    slot = jnp.sum(jnp.where(same, 1.0, 0.0), axis=0, keepdims=True).astype(jnp.int32)
    target = dest_row[...] * CAP + slot
    q = out.shape[0] * CAP
    selector = jnp.where(lax.broadcasted_iota(jnp.int32, (q, n), 0) == target, 1.0, 0.0).astype(BF16)
    height = fluid.shape[0]
    picked = jnp.where(lax.broadcasted_iota(jnp.int32, (height, n), 0) == rows[...], 1.0, 0.0)
    chosen = lax.dot_general(
        selector, picked.astype(BF16), (((1,), (1,)), ((), ())), preferred_element_type=F32
    ).astype(BF16)
    value = fluid[...]
    high = value.astype(BF16)
    rest = value - high.astype(F32)
    mid = rest.astype(BF16)
    low = (rest - mid.astype(F32)).astype(BF16)
    value = mul(chosen, high) + (mul(chosen, mid) + mul(chosen, low))
    out[...] = value.reshape(out.shape)


def turn_kernel(place, struct, fluid, own_s, send_s, own_f, send_f, held_s, held_f):
    core = place[3]
    held_s[...] = struct[...].T.reshape(held_s.shape)
    held_f[...] = fluid[...].T.reshape(held_f.shape)
    own_s[...] = held_s[:, core]
    send_s[...] = held_s[:, 1 - core]
    own_f[...] = held_f[:, core]
    send_f[...] = held_f[:, 1 - core]


def wet_kernel(coupling, received, out):
    right = received[...].reshape(coupling.shape[1], R)
    out[...] = product(parts(coupling[...]), parts(right))


def gathered(tiles, cols, total, at):
    total[:, at : at + TILE * tiles.shape[0]] = jnp.zeros(
        (total.shape[0], TILE * tiles.shape[0], TILE), F32
    )
    for i in range(tiles.shape[0]):
        rows = pl.ds(at + i * TILE, TILE)
        for k in range(tiles.shape[1]):
            c = cols[i, k]
            total[c, rows] = total[c, rows] + tiles[i, k]


def image(total, pieces):
    acc = None
    c = 0
    for piece in pieces:
        n = piece.shape[0] // TILE
        left = jnp.concatenate([total[c + i] for i in range(n)], axis=1) if n > 1 else total[c]
        term = product(parts(left), parts(piece))
        acc = term if acc is None else acc + term
        c += n
    return acc


def fluid_kernel(cols, stiff, mass, lo, own, hi, after, out, total):
    gathered(stiff, cols, total, 0)
    gathered(mass, cols, total, TILE)
    out[...] = image(total, (lo[...], own[...], hi[...])).reshape(out.shape)


def struct_kernel(cols, stiff, mass, lo, own, hi, after, out, total):
    gathered(stiff, cols, total, 0)
    gathered(mass, cols, total, 2 * TILE)
    out[...] = image(total, (lo[...], own[...], hi[...])).reshape(out.shape)


def joined(one, two):
    return jnp.concatenate([one[...].reshape(R // 2, -1), two[...].reshape(R // 2, -1)], axis=1)


def multiply(held, left, one, two):
    right = jnp.concatenate([one, two], axis=0)
    held[...] = product((left[0][...], left[1][...]), parts(right)).reshape(held.shape)


def send_off(place, held, outs):
    for o in range(4):
        dx = lax.rem(place[0] + o, 4)
        dy = lax.rem(place[1] + o, 4)
        for h in range(2):
            outs[o][0, h] = held[h * 4 + dx, 0:HALF, :]
        outs[4 + o][0] = held[:, HALF:, pl.ds(pl.multiple_of(dy * 256, 256), 256)]


def fluid_product_kernel(place, lf0, lf1, if0, if1, *rest):
    outs, (fh, fl, held) = rest[:8], rest[8:]

    @pl.when(pl.program_id(0) == 0)
    def _():
        fh[...], fl[...] = parts(joined(lf0, lf1))

    multiply(held, (fh, fl), if0[0], if1[0])
    send_off(place, held, outs)


def wet_product_kernel(place, ls0, ls1, ic0, ic1, *rest):
    outs, (sh, sl, held) = rest[8:16], rest[16:]
    sh[...], sl[...] = parts(joined(ls0, ls1))
    multiply(held, (sh, sl), ic0[...], ic1[...])
    send_off(place, held, outs)


def second_kernel(place, ls0, ls1, is0, is1, *rest):
    outs, (sh, sl, held) = rest[:8], rest[8:]

    @pl.when(pl.program_id(0) == 0)
    def _():
        sh[...], sl[...] = parts(joined(ls0, ls1))

    multiply(held, (sh, sl), is0[0], is1[0])
    send_off(place, held, outs)


def split_kernel(axis, place, a0, a1, a2, a3, o0, o1, o2, o3, held):
    held[...] = (a0[...] + a1[...]) + (a2[...] + a3[...])
    for o, out in enumerate((o0, o1, o2, o3)):
        d = lax.rem(place[axis] + o, 4)
        if axis == 1:
            out[...] = held[..., pl.ds(pl.multiple_of(d * 256, 256), 256)]
        else:
            for h in range(2):
                out[:, h] = held[:, h * 4 + d]


def spread_kernel(place, *refs):
    ins, outs, held = refs[:16], refs[16:20], refs[20]
    at = 0
    for x, y in ((ins[0:4], ins[4:8]), (ins[8:12], ins[12:16])):
        rows = slice(at, at + x[0].shape[0])
        held[rows, :, 0:HALF] = (x[0][...] + x[1][...]) + (x[2][...] + x[3][...])
        held[rows, :, HALF:] = (y[0][...] + y[1][...]) + (y[2][...] + y[3][...])
        at = rows.stop
    for o, out in enumerate(outs):
        d = lax.rem(place[2] + o, 4)
        lanes = pl.ds(pl.multiple_of(lax.rem(d, 2) * 128, 128), 128)
        out[...] = held[:, d // 2, :, lanes]


def last_kernel(a0, a1, a2, a3, *outs):
    for m, out in enumerate(outs):
        out[...] = (a0[m] + a1[m]) + (a2[m] + a3[m])


def call(kernel, out, count, smem=0, anywhere=0, scratch=(), flops=0, moved=0):
    run = pl.pallas_call(
        kernel,
        out_shape=out,
        in_specs=[SMEM] * smem + [VMEM] * (count - smem - anywhere) + [ANY] * anywhere,
        out_specs=jax.tree.map(lambda _: VMEM, out),
        scratch_shapes=list(scratch),
        compiler_params=PARAMS,
        cost_estimate=pl.CostEstimate(flops=flops, bytes_accessed=moved, transcendentals=0),
    )
    return run


def exchanged(slots, axis):
    return [slots[0]] + [shifted(slots[o], axis, o) for o in range(1, 4)]


def split(place, arrived, axis):
    count = arrived[0].shape[0]
    size = arrived[0].size
    return call(
        functools.partial(split_kernel, axis),
        [shape(count, 2, HALF, 256)] * 4,
        5,
        smem=1,
        scratch=[pltpu.VMEM(arrived[0].shape, F32)],
        flops=3 * size,
        moved=20 * size,
    )(place, *arrived)


def spread(place, *arrived):
    return call(
        spread_kernel,
        [shape(5, 64, 128)] * 4,
        17,
        smem=1,
        scratch=[pltpu.VMEM((5, 2, 64, 256), F32)],
        flops=2**20,
        moved=2**22,
    )(place, *arrived)


def partial_sums(kernel, steps, at, count, place, lefts, depth, operands, specs, carried=()):
    left = pltpu.VMEM((512, depth), BF16)
    run = pl.pallas_call(
        kernel,
        grid=(steps,),
        out_shape=[shape(count, 2, HALF, R)] * 4 + [shape(count, 8, HALF, 256)] * 4,
        in_specs=[SMEM] + [VMEM] * len(lefts) + specs + [ANY] * len(carried),
        out_specs=[pl.BlockSpec((1, 2, HALF, R), lambda m: (m + at, 0, 0, 0))] * 4
        + [pl.BlockSpec((1, 8, HALF, 256), lambda m: (m + at, 0, 0, 0))] * 4,
        scratch_shapes=[left, left, pltpu.VMEM((8, 64, R), F32)],
        input_output_aliases={1 + len(lefts) + len(specs) + i: i for i in range(len(carried))},
        compiler_params=PARAMS,
        cost_estimate=pl.CostEstimate(
            flops=6 * steps * 512 * depth * R, bytes_accessed=4 * steps * 2**20, transcendentals=0
        ),
    )
    return run(place, *lefts, *operands, *carried)


def compute(
    struct_basis,
    fluid_basis,
    stiff_tiles,
    mass_tiles,
    fluid_stiff_tiles,
    fluid_mass_tiles,
    struct_cols,
    fluid_cols,
    wet_rows,
    wet_dest,
    coupling,
):
    place = jnp.stack([lax.axis_index(X), lax.axis_index(Y), lax.axis_index(Z), lax.axis_index("core")]).astype(
        jnp.int32
    )
    tail, head = lax.optimization_barrier((struct_basis[-TILE:], struct_basis[:TILE]))
    below_s = from_behind(tail, 1)
    above_s = from_behind(head, -1)
    below_f = from_behind(fluid_basis, 1)
    above_f = from_behind(fluid_basis, -1)

    outgoing = call(route_kernel, shape(128, CAP, R), 3, flops=2 * 3 * 256 * 128 * R, moved=2**21)(
        wet_dest.reshape(1, -1), wet_rows.reshape(1, -1), fluid_basis
    )
    received = lax.all_to_all(outgoing, AXES, split_axis=0, concat_axis=0, tiled=True)

    own_s, send_s, own_f, send_f = call(
        turn_kernel,
        [shape(8, 64, 256)] * 2 + [shape(8, 64, 128)] * 2,
        3,
        smem=1,
        scratch=[pltpu.VMEM((8, 2, 64, 256), F32), pltpu.VMEM((8, 2, 64, 128), F32)],
        flops=2**20,
        moved=3 * 2**20,
    )(place, struct_basis, fluid_basis)
    left_s = shifted(send_s, "core", 1)
    left_f = shifted(send_f, "core", 1)

    image_c = call(wet_kernel, shape(256, R), 2, flops=6 * 256 * 256 * R, moved=2**21)(coupling, received)
    other_c = shifted(image_c, "core", 1)

    image_f = call(
        fluid_kernel,
        shape(2, 128, R),
        7,
        smem=1,
        anywhere=1,
        scratch=[pltpu.VMEM((3, 256, TILE), F32)],
        flops=6 * 256 * 384 * R,
        moved=3 * 2**20,
    )(fluid_cols, fluid_stiff_tiles, fluid_mass_tiles, below_f, fluid_basis, above_f, own_s)
    other_f = shifted(image_f, "core", 1)

    def block(rows):
        return pl.BlockSpec((1, rows, R), lambda m: (m, 0, 0))

    fluid = partial_sums(
        fluid_product_kernel, 2, 0, 3, place, (own_f, left_f), 256, (image_f, other_f), [block(128)] * 2
    )
    first = partial_sums(
        wet_product_kernel, 1, 2, 3, place, (own_s, left_s), 512, (image_c, other_c), [VMEM] * 2, fluid
    )
    first_x = exchanged(first[0:4], X)
    first_y = exchanged(first[4:8], Y)

    image_s = call(
        struct_kernel,
        shape(2, 256, R),
        7,
        smem=1,
        anywhere=1,
        scratch=[pltpu.VMEM((4, 512, TILE), F32)],
        flops=6 * 512 * 512 * R,
        moved=5 * 2**20,
    )(struct_cols, stiff_tiles, mass_tiles, below_s, struct_basis, above_s, first[0])
    other_s = shifted(image_s, "core", 1)

    second = partial_sums(second_kernel, 2, 0, 2, place, (own_s, left_s), 512, (image_s, other_s), [block(256)] * 2)
    second_x = exchanged(second[0:4], X)
    second_y = exchanged(second[4:8], Y)

    first_xy = exchanged(split(place, first_x, 1), Y)
    first_yx = exchanged(split(place, first_y, 0), X)
    second_xy = exchanged(split(place, second_x, 1), Y)
    second_yx = exchanged(split(place, second_y, 0), X)
    summed = exchanged(spread(place, *first_xy, *first_yx, *second_xy, *second_yx), Z)
    fstiff, fmass, wet, stiff, mass = call(last_kernel, [shape(64, 128)] * 5, 4, flops=2**18, moved=2**20)(*summed)
    return stiff, mass, fstiff, fmass, wet


def solution(mesh):
    fine = Mesh(mesh.devices.reshape(2, 4, 2, 4, 2), AXES)
    return jax.shard_map(
        compute,
        mesh=fine,
        in_specs=(
            P(AXES, None),
            P(AXES, None),
            P(AXES, None, None, None),
            P(AXES, None, None, None),
            P(AXES, None, None, None),
            P(AXES, None, None, None),
            P(AXES, None),
            P(AXES, None),
            P(AXES),
            P(AXES, None),
            P(AXES, None),
        ),
        out_specs=(P(ROW, COL),) * 5,
        check_vma=False,
    )
```
